256 devices in a mesh: blk: 32 (over z_lo, x, core), grp: 8 (over z_hi, y).
Axes of the slice: x: 4, y: 4, z: 8 (z_hi: 2, z_lo: 4; z = z_hi * 4 + z_lo), core: 2. Of those that a mesh axis runs over, the one named last changes fastest.
Arguments:
- lambda_init: float32 [131072, 256], P('blk'), may hold values from 0.1 to 200
- gamma_init: float32 [32768, 256], P(('blk', 'grp')), may hold values from 0.5 to 20
- dmr_table: float32 [1024, 256], replicated, may hold values from -3 to 3
- features: int32 [32768, 4], P(('blk', 'grp')), may hold values from 0 to 1023
- counts: int32 [256, 4, 6, 128, 128], P(('blk', 'grp')), may hold values from 0 to 3
- tile_cols: int32 [256, 4, 6], P(('blk', 'grp')), may hold values from 0 to 31, as said below
- live_slots: int32 [256, 4], P(('blk', 'grp')), may hold values from 1 to 6, as said below
Outputs:
- gamma_out: float32 [32768, 256], P(('blk', 'grp'))
- lambda_out: float32 [131072, 256], P(('blk', 'grp'))
The draws below stay inside these ranges and needn't reach their ends.
Inputs may be any that keep to these rules, and one draw needn't show every extreme that they name: `tile_cols`: within one row tile and substep the 6 column tiles are distinct. Slots 0 to live_slots - 1 of a row tile and substep are in use, the others are padding; row tile 0 uses all 6 slots in substep 0.
All inputs are finite; a program needn't handle non-finite values.
Results may differ from the reference program's by a relative error of at most 0.009.
Values sent between devices are 32-bit elements; how exact they have to be, the bound alone decides.
A program may use at most 128 MiB of HBM per device.

```python
import math
import jax
import jax.numpy as jnp
from jax import lax

TOPICS = 256
PANEL = 4096
TILE = 128
DOC_DEV = 128
SLOTS = 6
STRATA = 4
LOCAL = 3
FEAT_IDS = 1024
PER_DOC = 4
VOCAB = 131072
DOCS = 32768
ROW_TILES = 256
N_BLK = 32
N_GRP = 8


def draw_lambda_init(key, part):
    first, second = jax.random.split(key)
    base = jax.random.uniform(first, (VOCAB, TOPICS), jnp.float32, 0.5, 2.0)
    tile_scale = jnp.exp(jax.random.uniform(second, (VOCAB // TILE, 1, TOPICS), jnp.float32, 0.0, 2.3))
    rising = 1.0 + 2.0 * jnp.arange(VOCAB, dtype=jnp.float32) / VOCAB
    spread = jnp.broadcast_to(tile_scale, (VOCAB // TILE, TILE, TOPICS)).reshape(VOCAB, TOPICS)
    return (base * spread * rising[:, None]).astype(jnp.float32)


def draw_tile_cols(key, part):
    columns = PANEL // TILE
    scores = jax.random.randint(key, (ROW_TILES, STRATA, columns), 0, 1048576) * columns
    scores = scores + jnp.arange(columns, dtype=jnp.int32)[None, None, :]
    order = jnp.argsort(scores, axis=-1)
    return order[:, :, :SLOTS].astype(jnp.int32)


def draw_live_slots(key, part):
    first, second = jax.random.split(key)
    row_count = DOC_DEV // TILE
    level = jax.random.randint(first, (ROW_TILES // row_count,), 0, 4)
    level = jnp.repeat(level, row_count)
    upper = jnp.maximum(1, (level + 1) * SLOTS // 4)
    raw = jax.random.randint(second, (ROW_TILES, STRATA), 0, 1048576)
    live_count = 1 + raw % upper[:, None]
    live_count = live_count.at[0, 0].set(SLOTS)
    return live_count.astype(jnp.int32)


def plant(array, key, smallest, largest):
    shape = array.shape
    spot = [jax.random.randint(jax.random.fold_in(key, axis), (), 0, shape[axis]) for axis in range(len(shape))]
    array = array.at[tuple(spot)].set(smallest)
    longest = shape.index(max(shape))
    spot[longest] = (spot[longest] + 1) % shape[longest]
    return array.at[tuple(spot)].set(largest)


def steps_of(own_key, extent, pieces, least, largest):
    def one(axis_at, blocks):
        draws = jax.random.uniform(jax.random.fold_in(jax.random.fold_in(own_key, 6), axis_at), (blocks,), jnp.float32, least / len(pieces), largest / len(pieces))
        return jnp.repeat(jnp.exp(draws), extent[axis_at] // blocks).reshape((-1,) + (1,) * (len(extent) - axis_at - 1))

    level = one(*pieces[0])
    for cut in pieces[1:]:
        level = level * one(*cut)
    return level


def gaussian(stream_key, shape, width, limit, kind=jnp.bfloat16):
    entries = width * jax.random.normal(stream_key, shape, jnp.float32)
    return jnp.clip(entries, min=-limit, max=limit).astype(kind)


def setup_inputs(seed: int = 0) -> dict:
    key_list = jax.random.split(jax.random.key(seed), 8)
    return {
        "lambda_init": draw_lambda_init(jax.random.fold_in(key_list[7], 71), 0),
        "gamma_init": jnp.clip(jnp.exp(math.log(20.0) - 3.6888795 * jax.random.uniform(key_list[1], (DOCS, TOPICS), jnp.float32) ** steps_of(key_list[1], (DOCS, TOPICS), ((0, 256),), -0.2, 0.2)), 0.5, 20.0),
        "dmr_table": gaussian(key_list[2], (FEAT_IDS, TOPICS), 0.5, 3.0, jnp.float32),
        "features": plant(jax.random.randint(key_list[3], (DOCS, PER_DOC), 0, FEAT_IDS), jax.random.fold_in(key_list[3], 1), 0, FEAT_IDS - 1).astype(jnp.int32),
        "counts": plant(jax.random.randint(key_list[4], (ROW_TILES, STRATA, SLOTS, TILE, TILE), 0, 4), jax.random.fold_in(key_list[4], 1), 0, 3).astype(jnp.int32),
        "tile_cols": draw_tile_cols(jax.random.fold_in(key_list[7], 71), 0),
        "live_slots": draw_live_slots(jax.random.fold_in(key_list[7], 71), 0),
    }


stratum_order = (0, 1, 3, 2)
step_weight = 0.5
word_prior = 0.05


def expected_theta(doc_gamma):
    return jnp.exp(lax.digamma(doc_gamma) - lax.digamma(jnp.sum(doc_gamma, axis=1, keepdims=True))).astype(jnp.bfloat16)


def block_update(doc_gamma, feature_rows, tile_counts, column_ids, live_count, beta_exp, dmr_table):
    rows, slots = column_ids.shape
    columns = PANEL // TILE
    doc_alpha = jnp.exp(jnp.sum(jnp.take(dmr_table, feature_rows, axis=0), axis=1))
    word_tiles = jnp.take(beta_exp.reshape(columns, TILE, TOPICS), column_ids.reshape(-1), axis=0)
    word_tiles = word_tiles.reshape(rows, slots, TILE, TOPICS).astype(jnp.float32)
    active = jnp.arange(slots)[None, :] < live_count[:, None]
    tile_weight = jnp.where(active[:, :, None, None], tile_counts, 0).astype(jnp.float32)

    def ratio_of(theta_exp):
        theta_rows = theta_exp.astype(jnp.float32).reshape(rows, TILE, TOPICS)
        denom = jnp.einsum("rdk,rswk->rsdw", theta_rows, word_tiles)
        return theta_rows, (tile_weight / denom).astype(jnp.bfloat16)

    for repeat in range(LOCAL):
        theta_exp = expected_theta(doc_gamma)
        theta_rows, count_ratio = ratio_of(theta_exp)
        contrib = jnp.einsum("rsdw,rswk->rdk", count_ratio.astype(jnp.float32), word_tiles)
        doc_gamma = doc_alpha + theta_exp.astype(jnp.float32) * contrib.reshape(doc_gamma.shape)
    theta_exp = expected_theta(doc_gamma)
    theta_rows, count_ratio = ratio_of(theta_exp)
    stat_tiles = jnp.einsum("rsdw,rdk->rswk", count_ratio.astype(jnp.float32), theta_rows)
    accumulated = jnp.zeros((columns, TILE, TOPICS), jnp.float32)
    accumulated = accumulated.at[column_ids.reshape(-1)].add(stat_tiles.reshape(rows * slots, TILE, TOPICS))
    partial_value = (beta_exp.astype(jnp.float32) * accumulated.reshape(PANEL, TOPICS)).astype(jnp.bfloat16)
    return doc_gamma, partial_value


def reference(lambda_init, gamma_init, dmr_table, features, counts, tile_cols, live_slots):
    row_count = DOC_DEV // TILE
    gamma_all = gamma_init.reshape(N_BLK, N_GRP, DOC_DEV, TOPICS)
    feature_all = features.reshape(N_BLK, N_GRP, DOC_DEV, PER_DOC)
    counts_all = counts.reshape(N_BLK, N_GRP, row_count, STRATA, SLOTS, TILE, TILE)
    cols_all = tile_cols.reshape(N_BLK, N_GRP, row_count, STRATA, SLOTS)
    live_all = live_slots.reshape(N_BLK, N_GRP, row_count, STRATA)

    def run_group(lambda_sum, group):
        doc_gamma = lax.dynamic_index_in_dim(gamma_all, group, 1, keepdims=False)
        feature_group = lax.dynamic_index_in_dim(feature_all, group, 1, keepdims=False)
        counts_group = lax.dynamic_index_in_dim(counts_all, group, 1, keepdims=False)
        cols_group = lax.dynamic_index_in_dim(cols_all, group, 1, keepdims=False)
        live_group = lax.dynamic_index_in_dim(live_all, group, 1, keepdims=False)
        topic_panel = lambda_init
        for substep in range(STRATA):
            stratum = stratum_order[substep]
            topic_totals = jnp.sum(topic_panel, axis=0)
            beta_exp = jnp.exp(lax.digamma(topic_panel) - lax.digamma(topic_totals)[None, :]).astype(jnp.bfloat16)
            partner = jnp.bitwise_xor(jnp.arange(N_BLK, dtype=jnp.int32), stratum).astype(jnp.int32)
            beta_blocks = jnp.take(beta_exp.reshape(N_BLK, PANEL, TOPICS), partner, axis=0)

            def one_block(items):
                return block_update(items[0], items[1], items[2], items[3], items[4], items[5], dmr_table)

            doc_gamma, partial_value = lax.map(one_block, (doc_gamma, feature_group, counts_group[:, :, substep], cols_group[:, :, substep], live_group[:, :, substep], beta_blocks))
            by_panel = jnp.take(partial_value, partner, axis=0).reshape(VOCAB, TOPICS).astype(jnp.float32)
            topic_panel = (1.0 - step_weight) * topic_panel + step_weight * (word_prior + N_GRP * by_panel)
        return lambda_sum + topic_panel, doc_gamma

    lambda_sum, gammas = lax.scan(run_group, jnp.zeros((VOCAB, TOPICS), jnp.float32), jnp.arange(N_GRP, dtype=jnp.int32))
    gamma_out = jnp.transpose(gammas, (1, 0, 2, 3)).reshape(DOCS, TOPICS)
    lambda_out = lambda_sum / N_GRP
    return gamma_out, lambda_out
```

```python
import jax
import jax.numpy as jnp
from jax import lax
from jax.experimental import pallas as pl
from jax.experimental.pallas import tpu as pltpu
from jax.sharding import PartitionSpec as P

STRATA = 4
LOCAL = 3
ORDER = (0, 1, 3, 2)
SLOTS = 6
TILE = 128
HALF = 64
TOPICS = 256
COLS = 32
VOCAB = 131072
GROUPS = 8
WORD_PRIOR = 0.05
NX, NZ, NY = 4, 4, 4
MESH = pl.DeviceIdType.MESH
NT = (((1,), (1,)), ((), ()))
TN = (((0,), (0,)), ((), ()))
FWD_F, UNM_F, FWD_K, MRG_F, UNM_K, MRG_K, ACROSS = range(7)


def flip(value, bits):
    if bits & 1:
        value = value + 1 - 2 * (value % 2)
    if bits & 2:
        value = value + 2 - 4 * ((value // 2) % 2)
    return value


def psi_parts(x):
    q = x * (x + 3.0)
    d = q * (q + 2.0)
    v = x + 3.5
    r = 1.0 / (v * d)
    rv = r * d
    second = (2.0 * x + 3.0) * (2.0 * q + 2.0) * (r * v)
    r2 = rv * rv
    first = v + rv * (1.0 / 24.0 + r2 * (-37.0 / 5760.0 + r2 * (10313.0 / 2903040.0)))
    return first, second


def psi_parts_wide(x):
    q = x * (x + 3.0)
    v = x + 3.5
    rv = 1.0 / v
    second = (2.0 * x + 3.0) * (2.0 / q) * ((q + 1.0) / (q + 2.0))
    r2 = rv * rv
    first = v + rv * (1.0 / 24.0 + r2 * (-37.0 / 5760.0 + r2 * (10313.0 / 2903040.0)))
    return first, second


def kernel(
    info, inv, lam_any, cnt_any, gam_any, alp_any,
    gout, lout,
    lam, cnt, alp, gbuf, wts, ebuf, beta, theta, ratio, part, ar_src, ar_one, ar_mid, ar_two, rbuf, rrecv,
    lam_sem, in_sem, ar1_s, ar1_r, ar2_s, ar2_r, mv_s, mv_r, rs_s, rs_r,
):
    blk = lax.axis_index("blk")
    grp = lax.axis_index("grp")
    core = blk % 2
    x = (blk // 2) % NX
    z = blk // (2 * NX)
    y = grp % NY
    zh = grp // NY

    def near(k):
        step, side = (k + 1) // 2, (k + 1) % 2
        other = core + 1 - 2 * core if side else core
        return ((z * NX + (x + step) % NX) * 2 + other, grp)

    def far(k):
        return ((((z + k + 1) % NZ) * NX + x) * 2 + core, grp)

    up = (blk, zh * NY + (y + 1) % NY)
    down = (blk, zh * NY + (y + NY - 1) % NY)
    across = (blk, (1 - zh) * NY + y)
    peers = [near(k) for k in range(7)] + [far(k) for k in range(3)] + [up, down, across]

    barrier = pltpu.get_barrier_semaphore()
    for peer in peers:
        pl.semaphore_signal(barrier, inc=1, device_id=peer, device_id_type=MESH)

    chunks = 4
    rows = 2 * COLS // chunks

    def lam_copy(i):
        return pltpu.make_async_copy(lam_any.at[pl.ds(i * rows, rows)], lam.at[pl.ds(i * rows, rows)], lam_sem.at[i])

    for i in range(chunks):
        lam_copy(i).start()
    own = [
        pltpu.make_async_copy(cnt_any.at[0], cnt.at[0], in_sem.at[0]),
        pltpu.make_async_copy(gam_any, gbuf.at[0], in_sem.at[1]),
        pltpu.make_async_copy(alp_any, alp.at[0], in_sem.at[2]),
    ]
    for copy in own:
        copy.start()

    def visit(t):
        return (flip(blk, ORDER[t]), grp)

    def cnt_move(t):
        return pltpu.make_async_remote_copy(cnt_any.at[t], cnt.at[t], mv_s.at[t], mv_r.at[t], device_id=visit(t), device_id_type=MESH)

    def alp_move(t):
        return pltpu.make_async_remote_copy(alp_any, alp.at[t], mv_s.at[4 + t], mv_r.at[4 + t], device_id=visit(t), device_id_type=MESH)

    def gam_move(t):
        bits = ORDER[t] ^ (ORDER[t + 1] if t + 1 < STRATA else 0)
        return pltpu.make_async_remote_copy(gbuf.at[t], gbuf.at[t + 1], mv_s.at[8 + t], mv_r.at[8 + t], device_id=(flip(blk, bits), grp), device_id_type=MESH)

    def one_copy(r, k):
        return pltpu.make_async_remote_copy(ar_src.at[r], ar_one.at[r, k], ar1_s.at[r, k], ar1_r.at[r, k], device_id=near(k), device_id_type=MESH)

    def two_copy(r, k):
        return pltpu.make_async_remote_copy(ar_mid.at[r], ar_two.at[r, k], ar2_s.at[r, k], ar2_r.at[r, k], device_id=far(k), device_id_type=MESH)

    def sum_start(r, value):
        ar_src[r] = value
        for k in range(7):
            one_copy(r, k).start()

    def sum_middle(r):
        total = ar_src[r]
        for k in range(7):
            one_copy(r, k).wait_recv()
            total = total + ar_one[r, k]
        ar_mid[r] = total
        for k in range(3):
            two_copy(r, k).start()

    def sum_end(r):
        total = ar_mid[r]
        for k in range(3):
            two_copy(r, k).wait_recv()
            total = total + ar_two[r, k]
        return total

    def exp_psi(t):
        decay = 0.5**t
        offset = WORD_PRIOR * (1.0 - decay)

        def tile_half(i, carry):
            c = info[t, i // 2]
            h = i % 2
            value = lam[c * 2 + h]
            for s in range(t):
                value = value + part[(s * (SLOTS + 1) + inv[s, c]) * 2 + h]
            first, second = psi_parts(value * decay + offset)
            ebuf[i] = first * jnp.exp(-second)
            return carry

        lax.fori_loop(0, 2 * SLOTS, tile_half, 0)

    def weigh(t):
        live = info[t, SLOTS]
        for j in range(SLOTS):
            keep = jnp.where(j < live, 1.0, 0.0).astype(jnp.float32)
            wts[j // 2, :, (j % 2) * TILE : (j % 2 + 1) * TILE] = cnt[t, j].astype(jnp.float32) * keep

    def scale_beta(totals):
        v = totals - 0.5
        scale = 1.0 / (v + (1.0 / 24.0) / v)
        for i in range(2 * SLOTS):
            beta[i // 4, (i % 4) * HALF : (i % 4 + 1) * HALF, :] = (ebuf[i] * scale).astype(jnp.bfloat16)

    def expect(t):
        for h in range(2):
            g = gbuf[t, h * HALF : (h + 1) * HALF, :]
            first, second = psi_parts(g)
            row_first, row_second = psi_parts_wide(jnp.sum(g, axis=1, keepdims=True))
            theta[h * HALF : (h + 1) * HALF, :] = (
                first * (1.0 / row_first) * jnp.exp(row_second - second)
            ).astype(jnp.bfloat16)
        th = theta[...]
        for p in range(3):
            denom = lax.dot_general(th, beta[p], NT, preferred_element_type=jnp.float32)
            ratio[p] = (wts[p] / denom).astype(jnp.bfloat16)

    def update(t):
        expect(t)
        contrib = jnp.dot(ratio[0], beta[0], preferred_element_type=jnp.float32)
        contrib = contrib + jnp.dot(ratio[1], beta[1], preferred_element_type=jnp.float32)
        contrib = contrib + jnp.dot(ratio[2], beta[2], preferred_element_type=jnp.float32)
        gbuf[t] = alp[t] + theta[...].astype(jnp.float32) * contrib

    def statistics(t):
        expect(t)
        th = theta[...]
        scale = float(2 ** (t + 3))
        total = jnp.zeros((HALF, TOPICS), jnp.float32)
        for p in range(3):
            stat = lax.dot_general(ratio[p], th, TN, preferred_element_type=jnp.float32)
            for i in range(4):
                piece = beta[p, i * HALF : (i + 1) * HALF, :].astype(jnp.float32) * stat[i * HALF : (i + 1) * HALF, :]
                piece = piece.astype(jnp.bfloat16).astype(jnp.float32)
                total = total + piece
                part[(t * (SLOTS + 1)) * 2 + p * 4 + i] = piece * scale
        return jnp.sum(total, axis=0, keepdims=True)

    acc = jnp.zeros((32, TOPICS), jnp.float32)
    for i in range(chunks):
        lam_copy(i).wait()

        def add_rows(n, acc, i=i):
            value = lam[i * rows + n]
            return acc + (value[:32] + value[32:])

        acc = lax.fori_loop(0, rows, add_rows, acc)
    zero = jnp.zeros((HALF, TOPICS), jnp.float32)
    for s in range(STRATA):
        for h in range(2):
            part[(s * (SLOTS + 1) + SLOTS) * 2 + h] = zero
    pl.semaphore_wait(barrier, len(peers))
    sum_start(0, jnp.sum(acc, axis=0, keepdims=True))
    for copy in own:
        copy.wait()
    exp_psi(0)
    sum_middle(0)
    for t in range(1, STRATA):
        cnt_move(t).start()
        alp_move(t).start()
    weigh(0)
    totals = sum_end(0)

    for t in range(STRATA):
        scale_beta(totals)
        lax.fori_loop(0, LOCAL, lambda n, carry, t=t: (update(t), carry)[1], 0)
        gam_move(t).start()
        sums = statistics(t)
        if t + 1 < STRATA:
            sum_start(t + 1, sums)
            exp_psi(t + 1)
            sum_middle(t + 1)
            cnt_move(t + 1).wait_recv()
            alp_move(t + 1).wait_recv()
            weigh(t + 1)
            gam_move(t).wait_recv()
            totals = 0.5 * totals + 0.5 * (WORD_PRIOR * VOCAB + GROUPS * sum_end(t + 1))

    give = 1 - zh
    keep = zh
    ups = (FWD_F, MRG_F, UNM_K)

    def rs_copy(kind, i):
        to = across if kind == ACROSS else up if kind in ups else down
        return pltpu.make_async_remote_copy(rbuf.at[kind, i], rrecv.at[kind, i], rs_s.at[kind, i], rs_r.at[kind, i], device_id=to, device_id_type=MESH)

    def gathered(side, step, i, h):
        c = side * 16 + ((y + step) % NY) * 4 + i
        value = part[inv[0, c] * 2 + h]
        for s in range(1, STRATA):
            value = value + part[(s * (SLOTS + 1) + inv[s, c]) * 2 + h]
        return value

    def each(body):
        lax.fori_loop(0, 4, lambda i, carry: (body(i), carry)[1], 0)

    def put(kind, i, side, step, received=()):
        for other in received:
            rs_copy(other, i).wait_recv()
        for h in range(2):
            part_rows = pl.ds(h * HALF, HALF)
            value = gathered(side, step, i, h)
            for other in received:
                value = value + rrecv[other, i, part_rows, :]
            rbuf[kind, i, part_rows, :] = value
        rs_copy(kind, i).start()

    def first_round(i):
        put(FWD_F, i, give, 2)
        put(UNM_F, i, give, 3)

    def last_round(i):
        for kind in (UNM_K, MRG_K, ACROSS):
            rs_copy(kind, i).wait_recv()
        for h in range(2):
            part_rows = pl.ds(h * HALF, HALF)
            value = gathered(keep, 0, i, h)
            for kind in (UNM_K, MRG_K, ACROSS):
                value = value + rrecv[kind, i, part_rows, :]
            start = lam[(grp * 4 + i) * 2 + h]
            lout[i, part_rows, :] = start * 0.0625 + (value * (1.0 / 128.0) + WORD_PRIOR * 0.9375)

    def middle_round(i):
        put(ACROSS, i, give, 0, (UNM_F, MRG_F))
        put(MRG_K, i, keep, 3, (FWD_K,))

    each(first_round)
    each(lambda i: put(FWD_K, i, keep, 2))
    each(lambda i: put(MRG_F, i, give, 1, (FWD_F,)))
    each(lambda i: put(UNM_K, i, keep, 1))
    each(middle_round)
    gam_move(STRATA - 1).wait_recv()
    gout[...] = gbuf[STRATA]
    each(last_round)

    for r in range(STRATA):
        for k in range(7):
            one_copy(r, k).wait_send()
        for k in range(3):
            two_copy(r, k).wait_send()
        gam_move(r).wait_send()
        if r > 0:
            cnt_move(r).wait_send()
            alp_move(r).wait_send()

    def drain(i):
        for kind in range(7):
            rs_copy(kind, i).wait_send()

    each(drain)


def on_device(lambda_init, gamma_init, dmr_table, features, counts, tile_cols, live_slots):
    doc_alpha = jnp.exp(jnp.sum(jnp.take(dmr_table, features, axis=0), axis=1))
    own = jnp.concatenate([tile_cols[0], live_slots[0][:, None], jnp.zeros((STRATA, 1), jnp.int32)], axis=1)
    blocks = range(lax.axis_size("blk"))
    rows = [own[0:1]] + [
        lax.ppermute(own[t : t + 1], "blk", [(d, d ^ ORDER[t]) for d in blocks]) for t in range(1, STRATA)
    ]
    info = jnp.concatenate(rows, axis=0)
    match = info[:, None, :SLOTS] == jnp.arange(COLS, dtype=jnp.int32)[None, :, None]
    inv = SLOTS + jnp.sum(jnp.where(match, jnp.arange(SLOTS, dtype=jnp.int32) - SLOTS, 0), axis=2)
    inv = inv.astype(jnp.int32)
    smem = pl.BlockSpec(memory_space=pltpu.SMEM)
    hbm = pl.BlockSpec(memory_space=pl.ANY)
    vmem = pl.BlockSpec(memory_space=pltpu.VMEM)
    f32, bf16 = jnp.float32, jnp.bfloat16
    dma = pltpu.SemaphoreType.DMA
    doc = (TILE, TOPICS)
    gamma_out, lambda_out = pl.pallas_call(
        kernel,
        out_shape=(jax.ShapeDtypeStruct(doc, f32), jax.ShapeDtypeStruct((4,) + doc, f32)),
        in_specs=[smem, smem, hbm, hbm, hbm, hbm],
        out_specs=(vmem, vmem),
        scratch_shapes=[
            pltpu.VMEM((2 * COLS, HALF, TOPICS), f32),
            pltpu.VMEM((STRATA, SLOTS, TILE, TILE), jnp.int32),
            pltpu.VMEM((STRATA,) + doc, f32),
            pltpu.VMEM((STRATA + 1,) + doc, f32),
            pltpu.VMEM((3, TILE, 2 * TILE), f32),
            pltpu.VMEM((2 * SLOTS, HALF, TOPICS), f32),
            pltpu.VMEM((3, 2 * TILE, TOPICS), bf16),
            pltpu.VMEM(doc, bf16),
            pltpu.VMEM((3, TILE, 2 * TILE), bf16),
            pltpu.VMEM((STRATA * (SLOTS + 1) * 2, HALF, TOPICS), f32),
            pltpu.VMEM((STRATA, 1, TOPICS), f32),
            pltpu.VMEM((STRATA, 7, 1, TOPICS), f32),
            pltpu.VMEM((STRATA, 1, TOPICS), f32),
            pltpu.VMEM((STRATA, 3, 1, TOPICS), f32),
            pltpu.VMEM((7, 4) + doc, f32),
            pltpu.VMEM((7, 4) + doc, f32),
            dma((4,)),
            dma((3,)),
            dma((STRATA, 7)),
            dma((STRATA, 7)),
            dma((STRATA, 3)),
            dma((STRATA, 3)),
            dma((12,)),
            dma((12,)),
            dma((7, 4)),
            dma((7, 4)),
        ],
        compiler_params=pltpu.CompilerParams(collective_id=0, has_side_effects=True),
        name="strata",
    )(
        info,
        inv,
        lambda_init.reshape(2 * COLS, HALF, TOPICS),
        counts[0],
        gamma_init,
        doc_alpha,
    )
    return gamma_out, lambda_out.reshape(4 * TILE, TOPICS)


def solution(mesh):
    placed = (
        P("blk", None),
        P(("blk", "grp"), None),
        P(),
        P(("blk", "grp"), None),
        P(("blk", "grp"), None, None, None, None),
        P(("blk", "grp"), None, None),
        P(("blk", "grp"), None),
    )
    return jax.shard_map(
        on_device,
        mesh=mesh,
        in_specs=placed,
        out_specs=(P(("blk", "grp"), None), P(("blk", "grp"), None)),
        check_vma=False,
    )
```

```python
import jax
import jax.numpy as jnp
from jax import lax
from jax.experimental import pallas as pl
from jax.experimental.pallas import tpu as pltpu
from jax.sharding import PartitionSpec as P

STRATA = 4
LOCAL = 3
ORDER = (0, 1, 3, 2)
SLOTS = 6
TILE = 128
HALF = 64
TOPICS = 256
COLS = 32
VOCAB = 131072
GROUPS = 8
WORD_PRIOR = 0.05
NX, NZ, NY = 4, 4, 4
MESH = pl.DeviceIdType.MESH
NT = (((1,), (1,)), ((), ()))
TN = (((0,), (0,)), ((), ()))
FWD_F, UNM_F, FWD_K, MRG_F, UNM_K, MRG_K, ACROSS = range(7)


def flip(value, bits):
    if bits & 1:
        value = value + 1 - 2 * (value % 2)
    if bits & 2:
        value = value + 2 - 4 * ((value // 2) % 2)
    return value


def psi_parts(x):
    q = x * (x + 3.0)
    d = q * (q + 2.0)
    v = x + 3.5
    r = 1.0 / (v * d)
    rv = r * d
    second = (2.0 * x + 3.0) * (2.0 * q + 2.0) * (r * v)
    r2 = rv * rv
    first = v + rv * (1.0 / 24.0 + r2 * (-37.0 / 5760.0 + r2 * (10313.0 / 2903040.0)))
    return first, second


def psi_parts_wide(x):
    q = x * (x + 3.0)
    v = x + 3.5
    rv = 1.0 / v
    second = (2.0 * x + 3.0) * (2.0 / q) * ((q + 1.0) / (q + 2.0))
    r2 = rv * rv
    first = v + rv * (1.0 / 24.0 + r2 * (-37.0 / 5760.0 + r2 * (10313.0 / 2903040.0)))
    return first, second


def kernel(
    lam_any, cnt_any, gam_any, tab_any, feat_any, cols_any, live_any,
    gout, lout,
    lam, tab, cnt, alp, gbuf, wts, ebuf, beta, theta, ratio, part, colv, livv, feat, cols, live, inv,
    ar_src, ar_one, ar_mid, ar_two, rbuf, rrecv,
    lam_sem, in_sem, id_s, id_r, ar1_s, ar1_r, ar2_s, ar2_r, mv_s, mv_r, rs_s, rs_r,
):
    blk = lax.axis_index("blk")
    grp = lax.axis_index("grp")
    core = blk % 2
    x = (blk // 2) % NX
    z = blk // (2 * NX)
    y = grp % NY
    zh = grp // NY

    def near(k):
        step, side = (k + 1) // 2, (k + 1) % 2
        other = core + 1 - 2 * core if side else core
        return ((z * NX + (x + step) % NX) * 2 + other, grp)

    def far(k):
        return ((((z + k + 1) % NZ) * NX + x) * 2 + core, grp)

    def flipped(bits):
        return (flip(blk, bits), grp)

    up = (blk, zh * NY + (y + 1) % NY)
    down = (blk, zh * NY + (y + NY - 1) % NY)
    across = (blk, (1 - zh) * NY + y)
    peers = [near(k) for k in range(7)] + [far(k) for k in range(3)] + [up, down, across]

    barrier = pltpu.get_barrier_semaphore()
    for peer in peers:
        pl.semaphore_signal(barrier, inc=1, device_id=peer, device_id_type=MESH)

    chunks = 4
    rows = 2 * COLS // chunks

    def lam_copy(i):
        return pltpu.make_async_copy(lam_any.at[pl.ds(i * rows, rows)], lam.at[pl.ds(i * rows, rows)], lam_sem.at[i])

    own_ids = [
        pltpu.make_async_copy(cols_any, cols.at[0], in_sem.at[0]),
        pltpu.make_async_copy(live_any, live.at[0], in_sem.at[1]),
    ]
    own_docs = [
        pltpu.make_async_copy(feat_any, feat, in_sem.at[2]),
        pltpu.make_async_copy(tab_any, tab, in_sem.at[3]),
        pltpu.make_async_copy(cnt_any.at[0], cnt.at[0], in_sem.at[4]),
        pltpu.make_async_copy(gam_any, gbuf.at[0], in_sem.at[5]),
    ]
    for copy in own_ids:
        copy.start()
    for i in range(chunks):
        lam_copy(i).start()
    for copy in own_docs:
        copy.start()

    def move(src, dst, n, bits):
        return pltpu.make_async_remote_copy(src, dst, mv_s.at[n], mv_r.at[n], device_id=flipped(bits), device_id_type=MESH)

    def cnt_move(t, second):
        tiles = pl.ds(4, 2) if second else pl.ds(0, 4)
        return move(cnt_any.at[t, tiles], cnt.at[t, tiles], 2 * t + second, ORDER[t])

    def alp_move(t):
        if t == 3:
            return move(alp.at[2], alp.at[3], 8 + t, ORDER[2] ^ ORDER[3])
        return move(alp.at[0], alp.at[t], 8 + t, ORDER[t])

    def gam_move(t):
        bits = ORDER[t] ^ (ORDER[t + 1] if t + 1 < STRATA else 0)
        return move(gbuf.at[t], gbuf.at[t + 1], 12 + t, bits)

    def id_moves(t):
        return [
            pltpu.make_async_remote_copy(cols_any, colv.at[t], id_s.at[t, 0], id_r.at[t, 0], device_id=flipped(ORDER[t]), device_id_type=MESH),
            pltpu.make_async_remote_copy(live_any, livv.at[t], id_s.at[t, 1], id_r.at[t, 1], device_id=flipped(ORDER[t]), device_id_type=MESH),
        ]

    def one_copy(r, k):
        return pltpu.make_async_remote_copy(ar_src.at[r], ar_one.at[r, k], ar1_s.at[r, k], ar1_r.at[r, k], device_id=near(k), device_id_type=MESH)

    def two_copy(r, k):
        return pltpu.make_async_remote_copy(ar_mid.at[r], ar_two.at[r, k], ar2_s.at[r, k], ar2_r.at[r, k], device_id=far(k), device_id_type=MESH)

    def sum_start(r, value):
        ar_src[r] = value
        for k in range(7):
            one_copy(r, k).start()

    def sum_middle(r):
        total = ar_src[r]
        for k in range(7):
            one_copy(r, k).wait_recv()
            total = total + ar_one[r, k]
        ar_mid[r] = total
        for k in range(3):
            two_copy(r, k).start()

    def sum_end(r):
        total = ar_mid[r]
        for k in range(3):
            two_copy(r, k).wait_recv()
            total = total + ar_two[r, k]
        return total

    def find_slots(s):
        ids = [cols[s, s, j] for j in range(SLOTS)]

        def column(i, carry):
            for n in range(4):
                c = i * 4 + n
                slot = SLOTS
                for j in range(SLOTS):
                    slot = jnp.where(ids[j] == c, j, slot)
                inv[s, c] = slot
            return carry

        lax.fori_loop(0, COLS // 4, column, 0)

    def exp_psi(t):
        decay = 0.5**t
        offset = WORD_PRIOR * (1.0 - decay)

        def tile_half(i, carry):
            c = cols[t, t, i // 2]
            h = i % 2
            value = lam[c * 2 + h]
            for s in range(t):
                value = value + part[(s * (SLOTS + 1) + inv[s, c]) * 2 + h]
            first, second = psi_parts(value * decay + offset)
            ebuf[i] = first * jnp.exp(-second)
            return carry

        lax.fori_loop(0, 2 * SLOTS, tile_half, 0)

    def weigh(t):
        used = live[t, 0, t]
        for j in range(SLOTS):
            keep = jnp.where(j < used, 1.0, 0.0).astype(jnp.float32)
            wts[j // 2, :, (j % 2) * TILE : (j % 2 + 1) * TILE] = cnt[t, j].astype(jnp.float32) * keep

    def scale_beta(totals):
        v = totals - 0.5
        scale = 1.0 / (v + (1.0 / 24.0) / v)
        for i in range(2 * SLOTS):
            beta[i // 4, (i % 4) * HALF : (i % 4 + 1) * HALF, :] = (ebuf[i] * scale).astype(jnp.bfloat16)

    def doc_prior():
        def eight(b, carry):
            for r in range(8):
                n = b * 8 + r
                value = tab[pl.ds(feat[0, n], 1), :]
                for f in range(1, 4):
                    value = value + tab[pl.ds(feat[f, n], 1), :]
                alp[0, pl.ds(n, 1), :] = value
            return carry

        lax.fori_loop(0, TILE // 8, eight, 0)
        for h in range(2):
            alp[0, h * HALF : (h + 1) * HALF, :] = jnp.exp(alp[0, h * HALF : (h + 1) * HALF, :])

    def expect(t):
        for h in range(2):
            g = gbuf[t, h * HALF : (h + 1) * HALF, :]
            first, second = psi_parts(g)
            row_first, row_second = psi_parts_wide(jnp.sum(g, axis=1, keepdims=True))
            theta[h * HALF : (h + 1) * HALF, :] = (
                first * (1.0 / row_first) * jnp.exp(row_second - second)
            ).astype(jnp.bfloat16)

    def divide():
        th = theta[...]
        for p in range(3):
            denom = lax.dot_general(th, beta[p], NT, preferred_element_type=jnp.float32)
            ratio[p] = (wts[p] / denom).astype(jnp.bfloat16)

    def contribution():
        value = jnp.dot(ratio[0], beta[0], preferred_element_type=jnp.float32)
        value = value + jnp.dot(ratio[1], beta[1], preferred_element_type=jnp.float32)
        value = value + jnp.dot(ratio[2], beta[2], preferred_element_type=jnp.float32)
        return theta[...].astype(jnp.float32) * value

    def update(t):
        divide()
        gbuf[t] = alp[t] + contribution()
        expect(t)

    def statistics(t):
        th = theta[...]
        scale = float(2 ** (t + 3))
        for p in range(3):
            stat = lax.dot_general(ratio[p], th, TN, preferred_element_type=jnp.float32)
            for i in range(4):
                piece = beta[p, i * HALF : (i + 1) * HALF, :].astype(jnp.float32) * stat[i * HALF : (i + 1) * HALF, :]
                part[(t * (SLOTS + 1)) * 2 + p * 4 + i] = piece.astype(jnp.bfloat16).astype(jnp.float32) * scale

    acc = jnp.zeros((32, TOPICS), jnp.float32)
    for i in range(chunks):
        lam_copy(i).wait()

        def add_rows(n, acc, i=i):
            value = lam[i * rows + n]
            return acc + (value[:32] + value[32:])

        acc = lax.fori_loop(0, rows, add_rows, acc)
    sums = jnp.sum(acc, axis=0, keepdims=True)
    for copy in own_ids:
        copy.wait()
    pl.semaphore_wait(barrier, len(peers))
    sum_start(0, sums)
    for t in range(1, STRATA):
        for copy in id_moves(t):
            copy.start()
    exp_psi(0)
    zero = jnp.zeros((HALF, TOPICS), jnp.float32)
    for s in range(STRATA):
        for h in range(2):
            part[(s * (SLOTS + 1) + SLOTS) * 2 + h] = zero
    sum_middle(0)
    for t in (1, 2):
        cnt_move(t, 0).start()
    cnt_move(1, 1).start()
    for copy in own_docs:
        copy.wait()
    expect(0)
    weigh(0)
    doc_prior()
    alp_move(1).start()
    find_slots(0)
    for t in range(1, STRATA):
        for copy in id_moves(t):
            copy.wait_recv()
        local = [
            pltpu.make_async_copy(colv.at[t], cols.at[t], in_sem.at[0]),
            pltpu.make_async_copy(livv.at[t], live.at[t], in_sem.at[1]),
        ]
        for copy in local:
            copy.start()
        for copy in local:
            copy.wait()
    totals = sum_end(0)

    for t in range(STRATA):
        scale_beta(totals)
        lax.fori_loop(0, LOCAL, lambda n, carry, t=t: (update(t), carry)[1], 0)
        if t != 1:
            gam_move(t).start()
        divide()
        if t + 1 < STRATA:
            sum_start(t + 1, jnp.sum(contribution(), axis=0, keepdims=True))
        if t == 1:
            gam_move(t).start()
        if t == 2:
            cnt_move(3, 1).start()
        statistics(t)
        if t + 1 < STRATA:
            exp_psi(t + 1)
            sum_middle(t + 1)
            if t == 0:
                cnt_move(2, 1).start()
                alp_move(2).start()
            if t == 1:
                cnt_move(3, 0).start()
            find_slots(t + 1)
            alp_move(t + 1).wait_recv()
            if t == 1:
                alp_move(3).start()
            gam_move(t).wait_recv()
            expect(t + 1)
            cnt_move(t + 1, 0).wait_recv()
            cnt_move(t + 1, 1).wait_recv()
            weigh(t + 1)
            totals = 0.5 * totals + 0.5 * (WORD_PRIOR * VOCAB + GROUPS * sum_end(t + 1))

    give = 1 - zh
    keep = zh
    ups = (FWD_F, MRG_F, UNM_K)

    def rs_copy(kind, i):
        to = across if kind == ACROSS else up if kind in ups else down
        return pltpu.make_async_remote_copy(rbuf.at[kind, i], rrecv.at[kind, i], rs_s.at[kind, i], rs_r.at[kind, i], device_id=to, device_id_type=MESH)

    def gathered(side, step, i, h):
        c = side * 16 + ((y + step) % NY) * 4 + i
        value = part[inv[0, c] * 2 + h]
        for s in range(1, STRATA):
            value = value + part[(s * (SLOTS + 1) + inv[s, c]) * 2 + h]
        return value

    def put(kind, i, side, step, received=()):
        for other in received:
            rs_copy(other, i).wait_recv()
        for h in range(2):
            part_rows = pl.ds(h * HALF, HALF)
            value = gathered(side, step, i, h)
            for other in received:
                value = value + rrecv[other, i, part_rows, :]
            rbuf[kind, i, part_rows, :] = value
        rs_copy(kind, i).start()

    def each(body):
        lax.fori_loop(0, 4, lambda i, carry: (body(i), carry)[1], 0)

    def pair(first):
        put(FWD_F, first, give, 2)
        put(UNM_F, first, give, 3)

    def merge_give(i):
        put(MRG_F, i, give, 1, (FWD_F,))

    def merge_keep(i):
        put(MRG_K, i, keep, 3, (FWD_K,))

    def send_across(i):
        put(ACROSS, i, give, 0, (UNM_F, MRG_F))

    pair(0)
    pair(1)
    for i in (2, 3):
        put(UNM_F, i, give, 3)
    each(lambda i: put(FWD_K, i, keep, 2))
    merge_give(0)
    put(FWD_F, 2, give, 2)
    merge_give(1)
    put(FWD_F, 3, give, 2)
    send_across(0)
    merge_give(2)
    send_across(1)
    merge_keep(0)
    merge_give(3)
    each(lambda i: put(UNM_K, i, keep, 1))
    merge_keep(1)
    send_across(2)
    merge_keep(2)
    send_across(3)
    merge_keep(3)
    gam_move(STRATA - 1).wait_recv()
    gout[...] = gbuf[STRATA]

    def last_round(i):
        for kind in (UNM_K, MRG_K, ACROSS):
            rs_copy(kind, i).wait_recv()
        for h in range(2):
            part_rows = pl.ds(h * HALF, HALF)
            value = gathered(keep, 0, i, h)
            for kind in (UNM_K, MRG_K, ACROSS):
                value = value + rrecv[kind, i, part_rows, :]
            start = lam[(grp * 4 + i) * 2 + h]
            lout[i, part_rows, :] = start * 0.0625 + (value * (1.0 / 128.0) + WORD_PRIOR * 0.9375)

    each(last_round)

    for r in range(STRATA):
        for k in range(7):
            one_copy(r, k).wait_send()
        for k in range(3):
            two_copy(r, k).wait_send()
        gam_move(r).wait_send()
        if r > 0:
            cnt_move(r, 0).wait_send()
            cnt_move(r, 1).wait_send()
            alp_move(r).wait_send()
            for copy in id_moves(r):
                copy.wait_send()

    def drain(i):
        for kind in range(7):
            rs_copy(kind, i).wait_send()

    each(drain)


def on_device(lambda_init, gamma_init, dmr_table, features, counts, tile_cols, live_slots):
    hbm = pl.BlockSpec(memory_space=pl.ANY)
    vmem = pl.BlockSpec(memory_space=pltpu.VMEM)
    f32, bf16, i32 = jnp.float32, jnp.bfloat16, jnp.int32
    dma = pltpu.SemaphoreType.DMA
    doc = (TILE, TOPICS)
    gamma_out, lambda_out = pl.pallas_call(
        kernel,
        out_shape=(pltpu.VMEM(doc, f32), pltpu.VMEM((4,) + doc, f32)),
        in_specs=[hbm] * 7,
        out_specs=(vmem, vmem),
        scratch_shapes=[
            pltpu.VMEM((2 * COLS, HALF, TOPICS), f32),
            pltpu.VMEM((1024, TOPICS), f32),
            pltpu.VMEM((STRATA, SLOTS, TILE, TILE), i32),
            pltpu.VMEM((STRATA,) + doc, f32),
            pltpu.VMEM((STRATA + 1,) + doc, f32),
            pltpu.VMEM((3, TILE, 2 * TILE), f32),
            pltpu.VMEM((2 * SLOTS, HALF, TOPICS), f32),
            pltpu.VMEM((3, 2 * TILE, TOPICS), bf16),
            pltpu.VMEM(doc, bf16),
            pltpu.VMEM((3, TILE, 2 * TILE), bf16),
            pltpu.VMEM((STRATA * (SLOTS + 1) * 2, HALF, TOPICS), f32),
            pltpu.VMEM((STRATA, STRATA, SLOTS), i32),
            pltpu.VMEM((STRATA, 1, STRATA), i32),
            pltpu.SMEM((4, TILE), i32),
            pltpu.SMEM((STRATA, STRATA, SLOTS), i32),
            pltpu.SMEM((STRATA, 1, STRATA), i32),
            pltpu.SMEM((STRATA, COLS), i32),
            pltpu.VMEM((STRATA, 1, TOPICS), f32),
            pltpu.VMEM((STRATA, 7, 1, TOPICS), f32),
            pltpu.VMEM((STRATA, 1, TOPICS), f32),
            pltpu.VMEM((STRATA, 3, 1, TOPICS), f32),
            pltpu.VMEM((7, 4) + doc, f32),
            pltpu.VMEM((7, 4) + doc, f32),
            dma((4,)),
            dma((6,)),
            dma((STRATA, 2)),
            dma((STRATA, 2)),
            dma((STRATA, 7)),
            dma((STRATA, 7)),
            dma((STRATA, 3)),
            dma((STRATA, 3)),
            dma((16,)),
            dma((16,)),
            dma((7, 4)),
            dma((7, 4)),
        ],
        compiler_params=pltpu.CompilerParams(collective_id=0, has_side_effects=True),
        name="strata",
    )(
        lambda_init.reshape(2 * COLS, HALF, TOPICS),
        counts[0],
        gamma_init,
        dmr_table,
        features.T,
        tile_cols[0],
        live_slots,
    )
    return gamma_out, lambda_out.reshape(4 * TILE, TOPICS)


def solution(mesh):
    placed = (
        P("blk", None),
        P(("blk", "grp"), None),
        P(),
        P(("blk", "grp"), None),
        P(("blk", "grp"), None, None, None, None),
        P(("blk", "grp"), None, None),
        P(("blk", "grp"), None),
    )
    return jax.shard_map(
        on_device,
        mesh=mesh,
        in_specs=placed,
        out_specs=(P(("blk", "grp"), None), P(("blk", "grp"), None)),
        check_vma=False,
    )
```

```python
import jax
import jax.numpy as jnp
from jax import lax
from jax.experimental import pallas as pl
from jax.experimental.pallas import tpu as pltpu
from jax.sharding import PartitionSpec as P

STRATA = 4
LOCAL = 3
ORDER = (0, 1, 3, 2)
SLOTS = 6
TILE = 128
HALF = 64
TOPICS = 256
COLS = 32
VOCAB = 131072
GROUPS = 8
WORD_PRIOR = 0.05
NX, NZ, NY = 4, 4, 4
MESH = pl.DeviceIdType.MESH
NT = (((1,), (1,)), ((), ()))
TN = (((0,), (0,)), ((), ()))
PIECES = ((), ((0, 6),), ((0, 5), (5, 1)), ((0, 3), (3, 3)))
FWD_F, UNM_F, FWD_K, MRG_F, UNM_K, MRG_K, ACROSS = range(7)
FAR_FIRST = sorted(range(1, 2 * NX * NZ), key=lambda k: -(min(k // 2 % NX, NX - k // 2 % NX) + min(k // (2 * NX), NZ - k // (2 * NX))))


def flip(value, bits):
    if bits & 1:
        value = value + 1 - 2 * (value % 2)
    if bits & 2:
        value = value + 2 - 4 * ((value // 2) % 2)
    return value


def psi_parts(x):
    q = x * (x + 3.0)
    d = q * (q + 2.0)
    v = x + 3.5
    r = 1.0 / (v * d)
    rv = r * d
    second = (2.0 * x + 3.0) * (2.0 * q + 2.0) * (r * v)
    r2 = rv * rv
    first = v + rv * (1.0 / 24.0 + r2 * (-37.0 / 5760.0 + r2 * (10313.0 / 2903040.0)))
    return first, second


def psi_parts_wide(x):
    q = x * (x + 3.0)
    v = x + 3.5
    rv = 1.0 / v
    second = (2.0 * x + 3.0) * (2.0 / q) * ((q + 1.0) / (q + 2.0))
    r2 = rv * rv
    first = v + rv * (1.0 / 24.0 + r2 * (-37.0 / 5760.0 + r2 * (10313.0 / 2903040.0)))
    return first, second


def kernel(
    lam_any, cnt_any, gam_any, tab_any, feat_any, cols_any, live_any,
    gout, lout,
    lam, tab, cnt, alp, gbuf, wts, ebuf, beta, theta, ratio, part, colv, livv, featv, feat, cols, live, inv,
    ar_src, ar_dst, rbuf, rrecv,
    lam_sem, in_sem, id_s, id_r, ar_s, ar_r, mv_s, mv_r, rs_s, rs_r,
):
    blk = lax.axis_index("blk")
    grp = lax.axis_index("grp")
    core = blk % 2
    x = (blk // 2) % NX
    z = blk // (2 * NX)
    y = grp % NY
    zh = grp // NY

    def other(k):
        side = core + 1 - 2 * core if k % 2 else core
        return ((((z + k // (2 * NX)) % NZ) * NX + (x + (k // 2) % NX) % NX) * 2 + side, grp)

    others = [other(k) for k in FAR_FIRST]

    def flipped(bits):
        return (flip(blk, bits), grp)

    up = (blk, zh * NY + (y + 1) % NY)
    down = (blk, zh * NY + (y + NY - 1) % NY)
    across = (blk, (1 - zh) * NY + y)
    peers = others + [up, down, across]

    barrier = pltpu.get_barrier_semaphore()
    for peer in peers:
        pl.semaphore_signal(barrier, inc=1, device_id=peer, device_id_type=MESH)

    chunks = 4
    rows = 2 * COLS // chunks

    def lam_copy(i):
        return pltpu.make_async_copy(lam_any.at[pl.ds(i * rows, rows)], lam.at[pl.ds(i * rows, rows)], lam_sem.at[i])

    own_ids = [
        pltpu.make_async_copy(cols_any, cols.at[0], in_sem.at[0]),
        pltpu.make_async_copy(live_any, live.at[0], in_sem.at[1]),
    ]
    own_docs = [
        pltpu.make_async_copy(feat_any, feat, in_sem.at[2]),
        pltpu.make_async_copy(tab_any, tab, in_sem.at[3]),
        pltpu.make_async_copy(cnt_any.at[0], cnt.at[0], in_sem.at[4]),
        pltpu.make_async_copy(gam_any, gbuf.at[0], in_sem.at[5]),
    ]
    for copy in own_ids:
        copy.start()
    for i in range(chunks):
        lam_copy(i).start()
    for copy in own_docs:
        copy.start()

    def move(src, dst, n, bits):
        return pltpu.make_async_remote_copy(src, dst, mv_s.at[n], mv_r.at[n], device_id=flipped(bits), device_id_type=MESH)

    def cnt_move(t, n):
        tiles = pl.ds(*PIECES[t][n])
        return move(cnt_any.at[t, tiles], cnt.at[t, tiles], 3 * (t - 1) + n, ORDER[t])

    def alp_move(t):
        return move(alp.at[t - 1], alp.at[t], 8 + t, ORDER[t - 1] ^ ORDER[t])

    def feat_move():
        return move(feat_any, featv, 10, ORDER[2])

    def gam_move(t):
        bits = ORDER[t] ^ (ORDER[t + 1] if t + 1 < STRATA else 0)
        return move(gbuf.at[t], gbuf.at[t + 1], 12 + t, bits)

    def id_moves(t):
        return [
            pltpu.make_async_remote_copy(cols_any, colv.at[t], id_s.at[t, 0], id_r.at[t, 0], device_id=flipped(ORDER[t]), device_id_type=MESH),
            pltpu.make_async_remote_copy(live_any, livv.at[t], id_s.at[t, 1], id_r.at[t, 1], device_id=flipped(ORDER[t]), device_id_type=MESH),
        ]

    def sum_start(r, value):
        ar_src[r] = value
        for k, peer in enumerate(others):
            pltpu.make_async_remote_copy(ar_src.at[r], ar_dst.at[r, k], ar_s.at[r], ar_r.at[r], device_id=peer, device_id_type=MESH).start()

    def sum_wait(r, sem):
        pltpu.make_async_copy(ar_dst.at[r], ar_dst.at[r], sem.at[r]).wait()

    def sum_end(r):
        sum_wait(r, ar_r)
        parts = [ar_src[r]] + [ar_dst[r, k] for k in range(len(others))]
        while len(parts) > 1:
            parts = [sum(parts[i + 1 : i + 2], parts[i]) for i in range(0, len(parts), 2)]
        return parts[0]

    def find_slots(s):
        ids = [cols[s, s, j] for j in range(SLOTS)]

        def column(i, carry):
            for n in range(4):
                c = i * 4 + n
                slot = SLOTS
                for j in range(SLOTS):
                    slot = jnp.where(ids[j] == c, j, slot)
                inv[s, c] = slot
            return carry

        lax.fori_loop(0, COLS // 4, column, 0)

    def exp_psi(t):
        decay = 0.5**t
        offset = WORD_PRIOR * (1.0 - decay)

        def tile_half(i, carry):
            c = cols[t, t, i // 2]
            h = i % 2
            value = lam[c * 2 + h]
            for s in range(t):
                value = value + part[(s * (SLOTS + 1) + inv[s, c]) * 2 + h]
            first, second = psi_parts(value * decay + offset)
            ebuf[i] = first * jnp.exp(-second)
            return carry

        lax.fori_loop(0, 2 * SLOTS, tile_half, 0)

    def weigh(t):
        used = live[t, 0, t]
        for j in range(SLOTS):
            keep = jnp.where(j < used, 1.0, 0.0).astype(jnp.float32)
            wts[j // 2, :, (j % 2) * TILE : (j % 2 + 1) * TILE] = cnt[t, j].astype(jnp.float32) * keep

    def scale_beta(totals):
        v = totals - 0.5
        scale = 1.0 / (v + (1.0 / 24.0) / v)
        for i in range(2 * SLOTS):
            beta[i // 4, (i % 4) * HALF : (i % 4 + 1) * HALF, :] = (ebuf[i] * scale).astype(jnp.bfloat16)

    def doc_prior(t):
        def eight(b, carry):
            for r in range(8):
                n = b * 8 + r
                value = tab[pl.ds(feat[0, n], 1), :]
                for f in range(1, 4):
                    value = value + tab[pl.ds(feat[f, n], 1), :]
                alp[t, pl.ds(n, 1), :] = value
            return carry

        lax.fori_loop(0, TILE // 8, eight, 0)
        for h in range(2):
            alp[t, h * HALF : (h + 1) * HALF, :] = jnp.exp(alp[t, h * HALF : (h + 1) * HALF, :])

    def expect(t):
        for h in range(2):
            g = gbuf[t, h * HALF : (h + 1) * HALF, :]
            first, second = psi_parts(g)
            row_first, row_second = psi_parts_wide(jnp.sum(g, axis=1, keepdims=True))
            theta[h * HALF : (h + 1) * HALF, :] = (
                first * (1.0 / row_first) * jnp.exp(row_second - second)
            ).astype(jnp.bfloat16)

    def divide():
        th = theta[...]
        for p in range(3):
            denom = lax.dot_general(th, beta[p], NT, preferred_element_type=jnp.float32)
            ratio[p] = (wts[p] / denom).astype(jnp.bfloat16)

    def contribution():
        value = jnp.dot(ratio[0], beta[0], preferred_element_type=jnp.float32)
        value = value + jnp.dot(ratio[1], beta[1], preferred_element_type=jnp.float32)
        value = value + jnp.dot(ratio[2], beta[2], preferred_element_type=jnp.float32)
        return theta[...].astype(jnp.float32) * value

    def update(t):
        divide()
        gbuf[t] = alp[t] + contribution()
        expect(t)

    def statistics(t):
        th = theta[...]
        scale = float(2 ** (t + 3))
        for p in range(3):
            stat = lax.dot_general(ratio[p], th, TN, preferred_element_type=jnp.float32)
            for i in range(4):
                piece = beta[p, i * HALF : (i + 1) * HALF, :].astype(jnp.float32) * stat[i * HALF : (i + 1) * HALF, :]
                part[(t * (SLOTS + 1)) * 2 + p * 4 + i] = piece.astype(jnp.bfloat16).astype(jnp.float32) * scale

    acc = jnp.zeros((32, TOPICS), jnp.float32)
    for i in range(chunks):
        lam_copy(i).wait()

        def add_rows(n, acc, i=i):
            value = lam[i * rows + n]
            return acc + (value[:32] + value[32:])

        acc = lax.fori_loop(0, rows, add_rows, acc)
    sums = jnp.sum(acc, axis=0, keepdims=True)
    for copy in own_ids:
        copy.wait()
    pl.semaphore_wait(barrier, len(peers))
    sum_start(0, sums)
    for t in range(1, STRATA):
        for copy in id_moves(t):
            copy.start()
    feat_move().start()
    cnt_move(2, 0).start()
    cnt_move(1, 0).start()
    exp_psi(0)
    zero = jnp.zeros((HALF, TOPICS), jnp.float32)
    for s in range(STRATA):
        for h in range(2):
            part[(s * (SLOTS + 1) + SLOTS) * 2 + h] = zero
    for copy in own_docs:
        copy.wait()
    expect(0)
    weigh(0)
    doc_prior(0)
    alp_move(1).start()
    feat_move().wait_recv()
    next_feat = pltpu.make_async_copy(featv, feat, in_sem.at[2])
    next_feat.start()
    find_slots(0)
    for t in range(1, STRATA):
        for copy in id_moves(t):
            copy.wait_recv()
        local = [
            pltpu.make_async_copy(colv.at[t], cols.at[t], in_sem.at[0]),
            pltpu.make_async_copy(livv.at[t], live.at[t], in_sem.at[1]),
        ]
        for copy in local:
            copy.start()
        for copy in local:
            copy.wait()
    totals = sum_end(0)

    for t in range(STRATA):
        scale_beta(totals)
        lax.fori_loop(0, LOCAL, lambda n, carry, t=t: (update(t), carry)[1], 0)
        if t != 1:
            gam_move(t).start()
        divide()
        if t + 1 < STRATA:
            sum_start(t + 1, jnp.sum(contribution(), axis=0, keepdims=True))
        if t == 0:
            cnt_move(2, 1).start()
            cnt_move(3, 0).start()
        if t == 1:
            gam_move(t).start()
            cnt_move(3, 1).start()
        statistics(t)
        if t + 1 < STRATA:
            exp_psi(t + 1)
            find_slots(t + 1)
            if t == 0:
                next_feat.wait()
                doc_prior(2)
                alp_move(3).start()
            if t != 1:
                alp_move(t + 1).wait_recv()
            gam_move(t).wait_recv()
            expect(t + 1)
            for n in range(len(PIECES[t + 1])):
                cnt_move(t + 1, n).wait_recv()
            weigh(t + 1)
            totals = 0.5 * totals + 0.5 * (WORD_PRIOR * VOCAB + GROUPS * sum_end(t + 1))

    give = 1 - zh
    keep = zh
    ups = (FWD_F, MRG_F, UNM_K)

    def rs_copy(kind, i):
        to = across if kind == ACROSS else up if kind in ups else down
        return pltpu.make_async_remote_copy(rbuf.at[kind, i], rrecv.at[kind, i], rs_s.at[kind, i], rs_r.at[kind, i], device_id=to, device_id_type=MESH)

    def gathered(side, step, i, h):
        c = side * 16 + ((y + step) % NY) * 4 + i
        value = part[inv[0, c] * 2 + h]
        for s in range(1, STRATA):
            value = value + part[(s * (SLOTS + 1) + inv[s, c]) * 2 + h]
        return value

    def put(kind, i, side, step, received=()):
        for other in received:
            rs_copy(other, i).wait_recv()
        for h in range(2):
            part_rows = pl.ds(h * HALF, HALF)
            value = gathered(side, step, i, h)
            for other in received:
                value = value + rrecv[other, i, part_rows, :]
            rbuf[kind, i, part_rows, :] = value
        rs_copy(kind, i).start()

    def each(body):
        lax.fori_loop(0, 4, lambda i, carry: (body(i), carry)[1], 0)

    def pair(first):
        put(FWD_F, first, give, 2)
        put(UNM_F, first, give, 3)

    def merge_give(i):
        put(MRG_F, i, give, 1, (FWD_F,))

    def merge_keep(i):
        put(MRG_K, i, keep, 3, (FWD_K,))

    def send_across(i):
        put(ACROSS, i, give, 0, (UNM_F, MRG_F))

    pair(0)
    pair(1)
    for i in (2, 3):
        put(UNM_F, i, give, 3)
    each(lambda i: put(FWD_K, i, keep, 2))
    merge_give(0)
    put(FWD_F, 2, give, 2)
    merge_give(1)
    put(FWD_F, 3, give, 2)
    send_across(0)
    merge_give(2)
    send_across(1)
    merge_keep(0)
    merge_give(3)
    each(lambda i: put(UNM_K, i, keep, 1))
    merge_keep(1)
    send_across(2)
    merge_keep(2)
    send_across(3)
    merge_keep(3)
    gam_move(STRATA - 1).wait_recv()
    gout[...] = gbuf[STRATA]

    def last_round(i):
        for kind in (UNM_K, MRG_K, ACROSS):
            rs_copy(kind, i).wait_recv()
        for h in range(2):
            part_rows = pl.ds(h * HALF, HALF)
            value = gathered(keep, 0, i, h)
            for kind in (UNM_K, MRG_K, ACROSS):
                value = value + rrecv[kind, i, part_rows, :]
            start = lam[(grp * 4 + i) * 2 + h]
            lout[i, part_rows, :] = start * 0.0625 + (value * (1.0 / 128.0) + WORD_PRIOR * 0.9375)

    each(last_round)

    for r in range(STRATA):
        sum_wait(r, ar_s)
        gam_move(r).wait_send()
        if r > 0:
            if r == 2:
                feat_move().wait_send()
            else:
                alp_move(r).wait_send()
            for n in range(len(PIECES[r])):
                cnt_move(r, n).wait_send()
            for copy in id_moves(r):
                copy.wait_send()

    def drain(i):
        for kind in range(7):
            rs_copy(kind, i).wait_send()

    each(drain)


def on_device(lambda_init, gamma_init, dmr_table, features, counts, tile_cols, live_slots):
    hbm = pl.BlockSpec(memory_space=pl.ANY)
    vmem = pl.BlockSpec(memory_space=pltpu.VMEM)
    f32, bf16, i32 = jnp.float32, jnp.bfloat16, jnp.int32
    dma = pltpu.SemaphoreType.DMA
    doc = (TILE, TOPICS)
    gamma_out, lambda_out = pl.pallas_call(
        kernel,
        out_shape=(pltpu.VMEM(doc, f32), pltpu.VMEM((4,) + doc, f32)),
        in_specs=[hbm] * 7,
        out_specs=(vmem, vmem),
        scratch_shapes=[
            pltpu.VMEM((2 * COLS, HALF, TOPICS), f32),
            pltpu.VMEM((1024, TOPICS), f32),
            pltpu.VMEM((STRATA, SLOTS, TILE, TILE), i32),
            pltpu.VMEM((STRATA,) + doc, f32),
            pltpu.VMEM((STRATA + 1,) + doc, f32),
            pltpu.VMEM((3, TILE, 2 * TILE), f32),
            pltpu.VMEM((2 * SLOTS, HALF, TOPICS), f32),
            pltpu.VMEM((3, 2 * TILE, TOPICS), bf16),
            pltpu.VMEM(doc, bf16),
            pltpu.VMEM((3, TILE, 2 * TILE), bf16),
            pltpu.VMEM((STRATA * (SLOTS + 1) * 2, HALF, TOPICS), f32),
            pltpu.VMEM((STRATA, STRATA, SLOTS), i32),
            pltpu.VMEM((STRATA, 1, STRATA), i32),
            pltpu.VMEM((4, TILE), i32),
            pltpu.SMEM((4, TILE), i32),
            pltpu.SMEM((STRATA, STRATA, SLOTS), i32),
            pltpu.SMEM((STRATA, 1, STRATA), i32),
            pltpu.SMEM((STRATA, COLS), i32),
            pltpu.VMEM((STRATA, 1, TOPICS), f32),
            pltpu.VMEM((STRATA, len(FAR_FIRST), 1, TOPICS), f32),
            pltpu.VMEM((7, 4) + doc, f32),
            pltpu.VMEM((7, 4) + doc, f32),
            dma((4,)),
            dma((6,)),
            dma((STRATA, 2)),
            dma((STRATA, 2)),
            dma((STRATA,)),
            dma((STRATA,)),
            dma((16,)),
            dma((16,)),
            dma((7, 4)),
            dma((7, 4)),
        ],
        compiler_params=pltpu.CompilerParams(collective_id=0, has_side_effects=True),
        name="strata",
    )(
        lambda_init.reshape(2 * COLS, HALF, TOPICS),
        counts[0],
        gamma_init,
        dmr_table,
        features.T,
        tile_cols[0],
        live_slots,
    )
    return gamma_out, lambda_out.reshape(4 * TILE, TOPICS)


def solution(mesh):
    placed = (
        P("blk", None),
        P(("blk", "grp"), None),
        P(),
        P(("blk", "grp"), None),
        P(("blk", "grp"), None, None, None, None),
        P(("blk", "grp"), None, None),
        P(("blk", "grp"), None),
    )
    return jax.shard_map(
        on_device,
        mesh=mesh,
        in_specs=placed,
        out_specs=(P(("blk", "grp"), None), P(("blk", "grp"), None)),
        check_vma=False,
    )
```

```python
import jax
import jax.numpy as jnp
from jax import lax
from jax.experimental import pallas as pl
from jax.experimental.pallas import tpu as pltpu
from jax.sharding import PartitionSpec as P

STRATA = 4
LOCAL = 3
ORDER = (0, 1, 3, 2)
SLOTS = 6
TILE = 128
HALF = 64
TOPICS = 256
COLS = 32
VOCAB = 131072
GROUPS = 8
WORD_PRIOR = 0.05
NX, NZ, NY = 4, 4, 4
MESH = pl.DeviceIdType.MESH
NT = (((1,), (1,)), ((), ()))
TN = (((0,), (0,)), ((), ()))
PIECES = ((), ((0, 6),), ((0, 5), (5, 1)), ((0, 3), (3, 3)))
FWD_F, UNM_F, FWD_K, MRG_F, UNM_K, MRG_K, ACROSS = range(7)
FAR_FIRST = sorted(range(1, 2 * NX * NZ), key=lambda k: -(min(k // 2 % NX, NX - k // 2 % NX) + min(k // (2 * NX), NZ - k // (2 * NX))))


def flip(value, bits):
    if bits & 1:
        value = value + 1 - 2 * (value % 2)
    if bits & 2:
        value = value + 2 - 4 * ((value // 2) % 2)
    return value


def psi_parts(x):
    q = x * (x + 3.0)
    d = q * (q + 2.0)
    v = x + 3.5
    r = 1.0 / (v * d)
    rv = r * d
    second = 4.0 * ((x + 1.5) * (q + 1.0) * (r * v))
    r2 = rv * rv
    first = v + rv * (1.0 / 24.0 + r2 * (-37.0 / 5760.0 + r2 * (10313.0 / 2903040.0)))
    return first, second


def minus_psi(x):
    q = x * (x + 3.0)
    v = x + 3.5
    rv = 1.0 / v
    second = 4.0 * ((x + 1.5) * (q + 1.0)) * (1.0 / (q * (q + 2.0)))
    r2 = rv * rv
    first = v + rv * (1.0 / 24.0 + r2 * (-37.0 / 5760.0 + r2 * (10313.0 / 2903040.0)))
    return second - jnp.log(first)


def kernel(
    lam_any, cnt_any, gam_any, tab_any, feat_any, cols_any, live_any,
    gout, lout,
    lam, tab, cnt, alp, gbuf, wts, ebuf, beta, theta, rows_log, ratio, part, colv, livv, featv, feat, cols, live, inv,
    ar_src, ar_dst, rbuf, rrecv,
    lam_sem, in_sem, id_s, id_r, ar_s, ar_r, mv_s, mv_r, rs_s, rs_r,
):
    blk = lax.axis_index("blk")
    grp = lax.axis_index("grp")
    core = blk % 2
    x = (blk // 2) % NX
    z = blk // (2 * NX)
    y = grp % NY
    zh = grp // NY

    def other(k):
        side = core + 1 - 2 * core if k % 2 else core
        return ((((z + k // (2 * NX)) % NZ) * NX + (x + (k // 2) % NX) % NX) * 2 + side, grp)

    others = [other(k) for k in FAR_FIRST]

    def flipped(bits):
        return (flip(blk, bits), grp)

    up = (blk, zh * NY + (y + 1) % NY)
    down = (blk, zh * NY + (y + NY - 1) % NY)
    across = (blk, (1 - zh) * NY + y)
    peers = others + [up, down, across]

    barrier = pltpu.get_barrier_semaphore()
    for peer in peers:
        pl.semaphore_signal(barrier, inc=1, device_id=peer, device_id_type=MESH)

    chunks = 4
    rows = 2 * COLS // chunks

    def lam_copy(i):
        return pltpu.make_async_copy(lam_any.at[pl.ds(i * rows, rows)], lam.at[pl.ds(i * rows, rows)], lam_sem.at[i])

    own_ids = [
        pltpu.make_async_copy(cols_any, cols.at[0], in_sem.at[0]),
        pltpu.make_async_copy(live_any, live.at[0], in_sem.at[1]),
    ]
    own_docs = [
        pltpu.make_async_copy(feat_any, feat, in_sem.at[2]),
        pltpu.make_async_copy(tab_any, tab, in_sem.at[3]),
        pltpu.make_async_copy(cnt_any.at[0], cnt.at[0], in_sem.at[4]),
        pltpu.make_async_copy(gam_any, gbuf.at[0], in_sem.at[5]),
    ]
    for copy in own_ids:
        copy.start()
    for i in range(chunks):
        lam_copy(i).start()
    for copy in own_docs:
        copy.start()

    def move(src, dst, n, bits):
        return pltpu.make_async_remote_copy(src, dst, mv_s.at[n], mv_r.at[n], device_id=flipped(bits), device_id_type=MESH)

    def cnt_move(t, n):
        tiles = pl.ds(*PIECES[t][n])
        return move(cnt_any.at[t, tiles], cnt.at[t, tiles], 3 * (t - 1) + n, ORDER[t])

    def alp_move(t):
        return move(alp.at[t - 1], alp.at[t], 8 + t, ORDER[t - 1] ^ ORDER[t])

    def feat_move():
        return move(feat_any, featv, 10, ORDER[2])

    def gam_move(t):
        bits = ORDER[t] ^ (ORDER[t + 1] if t + 1 < STRATA else 0)
        return move(gbuf.at[t], gbuf.at[t + 1], 12 + t, bits)

    def id_moves(t):
        return [
            pltpu.make_async_remote_copy(cols_any, colv.at[t], id_s.at[t, 0], id_r.at[t, 0], device_id=flipped(ORDER[t]), device_id_type=MESH),
            pltpu.make_async_remote_copy(live_any, livv.at[t], id_s.at[t, 1], id_r.at[t, 1], device_id=flipped(ORDER[t]), device_id_type=MESH),
        ]

    def sum_start(r, value):
        ar_src[r] = value
        for k, peer in enumerate(others):
            pltpu.make_async_remote_copy(ar_src.at[r], ar_dst.at[r, k], ar_s.at[r], ar_r.at[r], device_id=peer, device_id_type=MESH).start()

    def sum_wait(r, sem):
        pltpu.make_async_copy(ar_dst.at[r], ar_dst.at[r], sem.at[r]).wait()

    def sum_end(r):
        sum_wait(r, ar_r)
        parts = [ar_src[r]] + [ar_dst[r, k] for k in range(len(others))]
        while len(parts) > 1:
            parts = [sum(parts[i + 1 : i + 2], parts[i]) for i in range(0, len(parts), 2)]
        return parts[0]

    def find_slots(s):
        ids = [cols[s, s, j] for j in range(SLOTS)]

        def column(i, carry):
            for n in range(4):
                c = i * 4 + n
                slot = SLOTS
                for j in range(SLOTS):
                    slot = jnp.where(ids[j] == c, j, slot)
                inv[s, c] = slot
            return carry

        lax.fori_loop(0, COLS // 4, column, 0)

    def exp_psi(t):
        decay = 0.5**t
        offset = WORD_PRIOR * (1.0 - decay)

        def tile_half(i, carry):
            c = cols[t, t, i // 2]
            h = i % 2
            value = lam[c * 2 + h]
            for s in range(t):
                value = value + part[(s * (SLOTS + 1) + inv[s, c]) * 2 + h]
            first, second = psi_parts(value * decay + offset)
            ebuf[i] = first * jnp.exp(-second)
            return carry

        lax.fori_loop(0, 2 * SLOTS, tile_half, 0)

    def weigh(t):
        used = live[t, 0, t]
        for j in range(SLOTS):
            keep = jnp.where(j < used, 1.0, 0.0).astype(jnp.float32)
            wts[j // 2, :, (j % 2) * TILE : (j % 2 + 1) * TILE] = cnt[t, j].astype(jnp.float32) * keep

    def scale_beta(totals):
        v = totals - 0.5
        scale = 1.0 / (v + (1.0 / 24.0) / v)
        for i in range(2 * SLOTS):
            beta[i // 4, (i % 4) * HALF : (i % 4 + 1) * HALF, :] = (ebuf[i] * scale).astype(jnp.bfloat16)

    def doc_prior(t):
        def eight(b, carry):
            for r in range(8):
                n = b * 8 + r
                value = tab[pl.ds(feat[0, n], 1), :]
                for f in range(1, 4):
                    value = value + tab[pl.ds(feat[f, n], 1), :]
                alp[t, pl.ds(n, 1), :] = value
            return carry

        lax.fori_loop(0, TILE // 8, eight, 0)
        for h in range(2):
            alp[t, h * HALF : (h + 1) * HALF, :] = jnp.exp(alp[t, h * HALF : (h + 1) * HALF, :])

    def row_sum(value):
        return jnp.sum(value, axis=1, keepdims=True)

    def set_rows(sums, h):
        rows_log[h * HALF : (h + 1) * HALF, :] = jnp.broadcast_to(minus_psi(sums), (HALF, TILE))

    def rows_arriving(t):
        for h in range(2):
            set_rows(row_sum(gbuf[t, h * HALF : (h + 1) * HALF, :]), h)

    def rows_staying(t):
        for h in range(2):
            docs = slice(h * HALF, (h + 1) * HALF)
            set_rows(row_sum(alp[t, docs, :]) + row_sum(wts[0, docs, :] + wts[1, docs, :] + wts[2, docs, :]), h)

    def expect(t):
        for h in range(2):
            docs = slice(h * HALF, (h + 1) * HALF)
            log_row = rows_log[docs, :]
            for side in range(2):
                topics = slice(side * TILE, (side + 1) * TILE)
                first, second = psi_parts(gbuf[t, docs, topics])
                theta[docs, topics] = (first * jnp.exp(log_row - second)).astype(jnp.bfloat16)

    def divide():
        th = theta[...]
        for p in range(3):
            denom = lax.dot_general(th, beta[p], NT, preferred_element_type=jnp.float32)
            ratio[p] = (wts[p] / denom).astype(jnp.bfloat16)

    def contribution():
        value = jnp.dot(ratio[0], beta[0], preferred_element_type=jnp.float32)
        value = value + jnp.dot(ratio[1], beta[1], preferred_element_type=jnp.float32)
        value = value + jnp.dot(ratio[2], beta[2], preferred_element_type=jnp.float32)
        return theta[...].astype(jnp.float32) * value

    def update(t):
        divide()
        gbuf[t] = alp[t] + contribution()
        expect(t)

    def statistics(t):
        th = theta[...]
        scale = float(2 ** (t + 3))
        for p in range(3):
            stat = lax.dot_general(ratio[p], th, TN, preferred_element_type=jnp.float32)
            for i in range(4):
                piece = beta[p, i * HALF : (i + 1) * HALF, :].astype(jnp.float32) * stat[i * HALF : (i + 1) * HALF, :]
                part[(t * (SLOTS + 1)) * 2 + p * 4 + i] = piece.astype(jnp.bfloat16).astype(jnp.float32) * scale

    acc = jnp.zeros((32, TOPICS), jnp.float32)
    for i in range(chunks):
        lam_copy(i).wait()

        def add_rows(n, acc, i=i):
            value = lam[i * rows + n]
            return acc + (value[:32] + value[32:])

        acc = lax.fori_loop(0, rows, add_rows, acc)
    sums = jnp.sum(acc, axis=0, keepdims=True)
    for copy in own_ids:
        copy.wait()
    pl.semaphore_wait(barrier, len(peers))
    sum_start(0, sums)
    for t in range(1, STRATA):
        for copy in id_moves(t):
            copy.start()
    feat_move().start()
    cnt_move(2, 0).start()
    cnt_move(1, 0).start()
    exp_psi(0)
    zero = jnp.zeros((HALF, TOPICS), jnp.float32)
    for s in range(STRATA):
        for h in range(2):
            part[(s * (SLOTS + 1) + SLOTS) * 2 + h] = zero
    for copy in own_docs:
        copy.wait()
    rows_arriving(0)
    expect(0)
    weigh(0)
    doc_prior(0)
    alp_move(1).start()
    feat_move().wait_recv()
    next_feat = pltpu.make_async_copy(featv, feat, in_sem.at[2])
    next_feat.start()
    find_slots(0)
    for t in range(1, STRATA):
        for copy in id_moves(t):
            copy.wait_recv()
        local = [
            pltpu.make_async_copy(colv.at[t], cols.at[t], in_sem.at[0]),
            pltpu.make_async_copy(livv.at[t], live.at[t], in_sem.at[1]),
        ]
        for copy in local:
            copy.start()
        for copy in local:
            copy.wait()
    rows_staying(0)
    totals = sum_end(0)

    for t in range(STRATA):
        scale_beta(totals)
        lax.fori_loop(0, LOCAL, lambda n, carry, t=t: (update(t), carry)[1], 0)
        if t != 1:
            gam_move(t).start()
        divide()
        if t + 1 < STRATA:
            sum_start(t + 1, jnp.sum(contribution(), axis=0, keepdims=True))
        if t == 0:
            cnt_move(2, 1).start()
            cnt_move(3, 0).start()
        if t == 1:
            gam_move(t).start()
            cnt_move(3, 1).start()
        statistics(t)
        if t + 1 < STRATA:
            exp_psi(t + 1)
            find_slots(t + 1)
            if t == 0:
                next_feat.wait()
                doc_prior(2)
                alp_move(3).start()
            if t != 1:
                alp_move(t + 1).wait_recv()
            gam_move(t).wait_recv()
            rows_arriving(t + 1)
            expect(t + 1)
            for n in range(len(PIECES[t + 1])):
                cnt_move(t + 1, n).wait_recv()
            weigh(t + 1)
            rows_staying(t + 1)
            totals = 0.5 * totals + 0.5 * (WORD_PRIOR * VOCAB + GROUPS * sum_end(t + 1))

    give = 1 - zh
    keep = zh
    ups = (FWD_F, MRG_F, UNM_K)
    ODD = 3

    def rs_copy(kind, i):
        to = across if kind == ACROSS else up if kind in ups else down
        return pltpu.make_async_remote_copy(rbuf.at[kind, i], rrecv.at[kind, i], rs_s.at[kind, i], rs_r.at[kind, i], device_id=to, device_id_type=MESH)

    def odd_copy(kind, h):
        if kind == FWD_F:
            return pltpu.make_async_remote_copy(rbuf.at[kind, ODD], rrecv.at[kind, ODD], rs_s.at[kind, ODD], rs_r.at[kind, ODD], device_id=across, device_id_type=MESH)
        rows_h = pl.ds(h * HALF, HALF)
        to = up if (kind == UNM_K) != (h == 1) else down
        return pltpu.make_async_remote_copy(rbuf.at[kind, ODD, rows_h], rrecv.at[kind, ODD, rows_h], rs_s.at[kind, ODD + h], rs_r.at[kind, ODD + h], device_id=to, device_id_type=MESH)

    def gathered(side, step, i, h):
        c = side * 16 + ((y + step) % NY) * 4 + i
        value = part[inv[0, c] * 2 + h]
        for s in range(1, STRATA):
            value = value + part[(s * (SLOTS + 1) + inv[s, c]) * 2 + h]
        return value

    def fill(kind, i, side, step, h, received=()):
        part_rows = pl.ds(h * HALF, HALF)
        value = gathered(side, step, i, h)
        for other in received:
            value = value + rrecv[other, i, part_rows, :]
        rbuf[kind, i, part_rows, :] = value

    def put(kind, i, side, step, received=()):
        for other in received:
            rs_copy(other, i).wait_recv()
        for h in range(2):
            fill(kind, i, side, step, h, received)
        rs_copy(kind, i).start()

    def first_three(body):
        lax.fori_loop(0, ODD, lambda i, carry: (body(i), carry)[1], 0)

    def merge_give(i):
        put(MRG_F, i, give, 1, (FWD_F,))

    def merge_keep(i):
        put(MRG_K, i, keep, 3, (FWD_K,))

    def send_across(i):
        put(ACROSS, i, give, 0, (UNM_F, MRG_F))

    for h in range(2):
        fill(FWD_F, ODD, give, 2, h)
    odd_copy(FWD_F, 0).start()
    put(MRG_F, ODD, give, 1)
    put(UNM_F, ODD, give, 3)
    for i in (0, 1):
        put(FWD_F, i, give, 2)
        put(UNM_F, i, give, 3)
    put(UNM_F, 2, give, 3)
    first_three(lambda i: put(FWD_K, i, keep, 2))
    send_across(ODD)
    merge_give(0)
    put(FWD_F, 2, give, 2)
    merge_give(1)
    send_across(0)
    merge_give(2)
    odd_copy(FWD_F, 0).wait_recv()
    for h in range(2):
        fill(FWD_K, ODD, keep, 2, h, (FWD_F,))
        odd_copy(FWD_K, h).start()
    first_three(lambda i: put(UNM_K, i, keep, 1))
    for h in range(2):
        fill(UNM_K, ODD, keep, 1 + 2 * h, h)
        odd_copy(UNM_K, h).start()
    merge_keep(0)
    send_across(1)
    merge_keep(1)
    merge_keep(2)
    send_across(2)
    for h in range(2):
        odd_copy(FWD_K, h).wait_recv()
        fill(MRG_K, ODD, keep, 3 - 2 * h, h, (FWD_K,))
        odd_copy(MRG_K, h).start()
    gam_move(STRATA - 1).wait_recv()
    gout[...] = gbuf[STRATA]

    def finish(i):
        for h in range(2):
            part_rows = pl.ds(h * HALF, HALF)
            value = gathered(keep, 0, i, h)
            for kind in (UNM_K, MRG_K, ACROSS):
                value = value + rrecv[kind, i, part_rows, :]
            start = lam[(grp * 4 + i) * 2 + h]
            lout[i, part_rows, :] = start * 0.0625 + (value * (1.0 / 128.0) + WORD_PRIOR * 0.9375)

    def last_round(i):
        for kind in (UNM_K, MRG_K, ACROSS):
            rs_copy(kind, i).wait_recv()
        finish(i)

    first_three(last_round)
    for h in range(2):
        odd_copy(UNM_K, h).wait_recv()
        odd_copy(MRG_K, h).wait_recv()
    rs_copy(ACROSS, ODD).wait_recv()
    finish(ODD)

    for r in range(STRATA):
        sum_wait(r, ar_s)
        gam_move(r).wait_send()
        if r > 0:
            if r == 2:
                feat_move().wait_send()
            else:
                alp_move(r).wait_send()
            for n in range(len(PIECES[r])):
                cnt_move(r, n).wait_send()
            for copy in id_moves(r):
                copy.wait_send()

    def drain(i):
        for kind in range(7):
            rs_copy(kind, i).wait_send()

    first_three(drain)
    for kind in (MRG_F, UNM_F, ACROSS):
        rs_copy(kind, ODD).wait_send()
    odd_copy(FWD_F, 0).wait_send()
    for kind in (FWD_K, MRG_K, UNM_K):
        for h in range(2):
            odd_copy(kind, h).wait_send()


def on_device(lambda_init, gamma_init, dmr_table, features, counts, tile_cols, live_slots):
    hbm = pl.BlockSpec(memory_space=pl.ANY)
    vmem = pl.BlockSpec(memory_space=pltpu.VMEM)
    f32, bf16, i32 = jnp.float32, jnp.bfloat16, jnp.int32
    dma = pltpu.SemaphoreType.DMA
    doc = (TILE, TOPICS)
    gamma_out, lambda_out = pl.pallas_call(
        kernel,
        out_shape=(pltpu.VMEM(doc, f32), pltpu.VMEM((4,) + doc, f32)),
        in_specs=[hbm] * 7,
        out_specs=(vmem, vmem),
        scratch_shapes=[
            pltpu.VMEM((2 * COLS, HALF, TOPICS), f32),
            pltpu.VMEM((1024, TOPICS), f32),
            pltpu.VMEM((STRATA, SLOTS, TILE, TILE), i32),
            pltpu.VMEM((STRATA,) + doc, f32),
            pltpu.VMEM((STRATA + 1,) + doc, f32),
            pltpu.VMEM((3, TILE, 2 * TILE), f32),
            pltpu.VMEM((2 * SLOTS, HALF, TOPICS), f32),
            pltpu.VMEM((3, 2 * TILE, TOPICS), bf16),
            pltpu.VMEM(doc, bf16),
            pltpu.VMEM((TILE, TILE), f32),
            pltpu.VMEM((3, TILE, 2 * TILE), bf16),
            pltpu.VMEM((STRATA * (SLOTS + 1) * 2, HALF, TOPICS), f32),
            pltpu.VMEM((STRATA, STRATA, SLOTS), i32),
            pltpu.VMEM((STRATA, 1, STRATA), i32),
            pltpu.VMEM((4, TILE), i32),
            pltpu.SMEM((4, TILE), i32),
            pltpu.SMEM((STRATA, STRATA, SLOTS), i32),
            pltpu.SMEM((STRATA, 1, STRATA), i32),
            pltpu.SMEM((STRATA, COLS), i32),
            pltpu.VMEM((STRATA, 1, TOPICS), f32),
            pltpu.VMEM((STRATA, len(FAR_FIRST), 1, TOPICS), f32),
            pltpu.VMEM((7, 4) + doc, f32),
            pltpu.VMEM((7, 4) + doc, f32),
            dma((4,)),
            dma((6,)),
            dma((STRATA, 2)),
            dma((STRATA, 2)),
            dma((STRATA,)),
            dma((STRATA,)),
            dma((16,)),
            dma((16,)),
            dma((7, 5)),
            dma((7, 5)),
        ],
        compiler_params=pltpu.CompilerParams(collective_id=0, has_side_effects=True),
        name="strata",
    )(
        lambda_init.reshape(2 * COLS, HALF, TOPICS),
        counts[0],
        gamma_init,
        dmr_table,
        features.T,
        tile_cols[0],
        live_slots,
    )
    return gamma_out, lambda_out.reshape(4 * TILE, TOPICS)


def solution(mesh):
    placed = (
        P("blk", None),
        P(("blk", "grp"), None),
        P(),
        P(("blk", "grp"), None),
        P(("blk", "grp"), None, None, None, None),
        P(("blk", "grp"), None, None),
        P(("blk", "grp"), None),
    )
    return jax.shard_map(
        on_device,
        mesh=mesh,
        in_specs=placed,
        out_specs=(P(("blk", "grp"), None), P(("blk", "grp"), None)),
        check_vma=False,
    )
```

```python
import jax
import jax.numpy as jnp
from jax import lax
from jax.experimental import pallas as pl
from jax.experimental.pallas import tpu as pltpu
from jax.sharding import PartitionSpec as P

STRATA = 4
LOCAL = 3
ORDER = (0, 1, 3, 2)
SLOTS = 6
TILE = 128
HALF = 64
TOPICS = 256
COLS = 32
VOCAB = 131072
GROUPS = 8
WORD_PRIOR = 0.05
NX, NZ, NY = 4, 4, 4
MESH = pl.DeviceIdType.MESH
NT = (((1,), (1,)), ((), ()))
TN = (((0,), (0,)), ((), ()))
PIECES = ((), ((0, 6),), ((0, 5), (5, 1)), ((0, 3), (3, 3)))
FWD_F, UNM_F, FWD_K, MRG_F, UNM_K, MRG_K, ACROSS = range(7)
FAR_FIRST = sorted(range(1, 2 * NX * NZ), key=lambda k: -(min(k // 2 % NX, NX - k // 2 % NX) + min(k // (2 * NX), NZ - k // (2 * NX))))


def flip(value, bits):
    if bits & 1:
        value = value + 1 - 2 * (value % 2)
    if bits & 2:
        value = value + 2 - 4 * ((value // 2) % 2)
    return value


def psi_parts(x):
    q = x * (x + 3.0)
    d = q * (q + 2.0)
    v = x + 3.5
    r = 1.0 / (v * d)
    rv = r * d
    second = 4.0 * ((x + 1.5) * (q + 1.0) * (r * v))
    r2 = rv * rv
    first = v + rv * (1.0 / 24.0 + r2 * (-37.0 / 5760.0 + r2 * (10313.0 / 2903040.0)))
    return first, second


def minus_psi(x):
    q = x * (x + 3.0)
    v = x + 3.5
    rv = 1.0 / v
    second = 4.0 * ((x + 1.5) * (q + 1.0)) * (1.0 / (q * (q + 2.0)))
    r2 = rv * rv
    first = v + rv * (1.0 / 24.0 + r2 * (-37.0 / 5760.0 + r2 * (10313.0 / 2903040.0)))
    return second - jnp.log(first)


def kernel(
    lam_any, cnt_any, gam_any, tab_any, feat_any, cols_any, live_any,
    gout, lout,
    lam, tab, cnt, alp, gbuf, wts, ebuf, beta, theta, rows_log, ratio, part, colv, livv, featv, feat, cols, live, inv,
    ar_src, ar_dst, rbuf, rrecv,
    lam_sem, in_sem, id_s, id_r, ar_s, ar_r, mv_s, mv_r, rs_s, rs_r,
):
    blk = lax.axis_index("blk")
    grp = lax.axis_index("grp")
    core = blk % 2
    x = (blk // 2) % NX
    z = blk // (2 * NX)
    y = grp % NY
    zh = grp // NY

    def other(k):
        side = core + 1 - 2 * core if k % 2 else core
        return ((((z + k // (2 * NX)) % NZ) * NX + (x + (k // 2) % NX) % NX) * 2 + side, grp)

    others = [other(k) for k in FAR_FIRST]

    def flipped(bits):
        return (flip(blk, bits), grp)

    up = (blk, zh * NY + (y + 1) % NY)
    down = (blk, zh * NY + (y + NY - 1) % NY)
    across = (blk, (1 - zh) * NY + y)
    peers = others + [up, down, across]

    barrier = pltpu.get_barrier_semaphore()
    for peer in peers:
        pl.semaphore_signal(barrier, inc=1, device_id=peer, device_id_type=MESH)

    chunks = 4
    rows = 2 * COLS // chunks

    def lam_copy(i):
        return pltpu.make_async_copy(lam_any.at[pl.ds(i * rows, rows)], lam.at[pl.ds(i * rows, rows)], lam_sem.at[i])

    own_ids = [
        pltpu.make_async_copy(cols_any, cols.at[0], in_sem.at[0]),
        pltpu.make_async_copy(live_any, live.at[0], in_sem.at[1]),
    ]
    own_docs = [
        pltpu.make_async_copy(feat_any, feat, in_sem.at[2]),
        pltpu.make_async_copy(tab_any, tab, in_sem.at[3]),
        pltpu.make_async_copy(cnt_any.at[0], cnt.at[0], in_sem.at[4]),
        pltpu.make_async_copy(gam_any, gbuf.at[0], in_sem.at[5]),
    ]
    for copy in own_ids:
        copy.start()
    for i in range(chunks):
        lam_copy(i).start()
    for copy in own_docs:
        copy.start()

    def move(src, dst, n, bits):
        return pltpu.make_async_remote_copy(src, dst, mv_s.at[n], mv_r.at[n], device_id=flipped(bits), device_id_type=MESH)

    def cnt_move(t, n):
        tiles = pl.ds(*PIECES[t][n])
        return move(cnt_any.at[t, tiles], cnt.at[t, tiles], 3 * (t - 1) + n, ORDER[t])

    def alp_move(t):
        return move(alp.at[t - 1], alp.at[t], 8 + t, ORDER[t - 1] ^ ORDER[t])

    def feat_move():
        return move(feat_any, featv, 10, ORDER[2])

    def gam_move(t, h):
        bits = ORDER[t] ^ (ORDER[t + 1] if t + 1 < STRATA else 0)
        rows_h = pl.ds(h * HALF, HALF)
        return move(gbuf.at[t, rows_h], gbuf.at[t + 1, rows_h], 12 + 2 * t + h, bits)

    def id_moves(t):
        return [
            pltpu.make_async_remote_copy(cols_any, colv.at[t], id_s.at[t, 0], id_r.at[t, 0], device_id=flipped(ORDER[t]), device_id_type=MESH),
            pltpu.make_async_remote_copy(live_any, livv.at[t], id_s.at[t, 1], id_r.at[t, 1], device_id=flipped(ORDER[t]), device_id_type=MESH),
        ]

    def sum_start(r, value):
        ar_src[r] = value
        for k, peer in enumerate(others):
            pltpu.make_async_remote_copy(ar_src.at[r], ar_dst.at[r, k], ar_s.at[r], ar_r.at[r], device_id=peer, device_id_type=MESH).start()

    def sum_wait(r, sem):
        pltpu.make_async_copy(ar_dst.at[r], ar_dst.at[r], sem.at[r]).wait()

    def sum_end(r):
        sum_wait(r, ar_r)
        parts = [ar_src[r]] + [ar_dst[r, k] for k in range(len(others))]
        while len(parts) > 1:
            parts = [sum(parts[i + 1 : i + 2], parts[i]) for i in range(0, len(parts), 2)]
        return parts[0]

    def find_slots(s):
        ids = [cols[s, s, j] for j in range(SLOTS)]

        def column(i, carry):
            for n in range(4):
                c = i * 4 + n
                slot = SLOTS
                for j in range(SLOTS):
                    slot = jnp.where(ids[j] == c, j, slot)
                inv[s, c] = slot
            return carry

        lax.fori_loop(0, COLS // 4, column, 0)

    def exp_psi(t):
        decay = 0.5**t
        offset = WORD_PRIOR * (1.0 - decay)

        def tile_half(i, carry):
            c = cols[t, t, i // 2]
            h = i % 2
            value = lam[c * 2 + h]
            for s in range(t):
                value = value + part[(s * (SLOTS + 1) + inv[s, c]) * 2 + h]
            first, second = psi_parts(value * decay + offset)
            ebuf[i] = first * jnp.exp(-second)
            return carry

        lax.fori_loop(0, 2 * SLOTS, tile_half, 0)

    def weigh(t):
        used = live[t, 0, t]
        for j in range(SLOTS):
            keep = jnp.where(j < used, 1.0, 0.0).astype(jnp.float32)
            wts[j // 2, :, (j % 2) * TILE : (j % 2 + 1) * TILE] = cnt[t, j].astype(jnp.float32) * keep

    def scale_beta(totals):
        v = totals - 0.5
        scale = v / (v * v + 1.0 / 24.0)
        for i in range(2 * SLOTS):
            beta[i // 4, (i % 4) * HALF : (i % 4 + 1) * HALF, :] = (ebuf[i] * scale).astype(jnp.bfloat16)

    def doc_prior(t):
        def eight(b, carry):
            for r in range(8):
                n = b * 8 + r
                value = tab[pl.ds(feat[0, n], 1), :]
                for f in range(1, 4):
                    value = value + tab[pl.ds(feat[f, n], 1), :]
                alp[t, pl.ds(n, 1), :] = value
            return carry

        lax.fori_loop(0, TILE // 8, eight, 0)
        for h in range(2):
            alp[t, h * HALF : (h + 1) * HALF, :] = jnp.exp(alp[t, h * HALF : (h + 1) * HALF, :])

    def row_sum(value):
        return jnp.sum(value, axis=1, keepdims=True)

    def set_rows(sums, h):
        rows_log[h * HALF : (h + 1) * HALF, :] = jnp.broadcast_to(minus_psi(sums), (HALF, TILE))

    def rows_arriving(t, h):
        set_rows(row_sum(gbuf[t, h * HALF : (h + 1) * HALF, :]), h)

    def rows_staying(t):
        for h in range(2):
            docs = slice(h * HALF, (h + 1) * HALF)
            set_rows(row_sum(alp[t, docs, :]) + row_sum(wts[0, docs, :] + wts[1, docs, :] + wts[2, docs, :]), h)

    def expect(t, *halves):
        for h in halves:
            docs = slice(h * HALF, (h + 1) * HALF)
            log_row = rows_log[docs, :]
            for side in range(2):
                topics = slice(side * TILE, (side + 1) * TILE)
                first, second = psi_parts(gbuf[t, docs, topics])
                theta[docs, topics] = (first * jnp.exp(log_row - second)).astype(jnp.bfloat16)

    def divide():
        th = theta[...]
        for p in range(3):
            denom = lax.dot_general(th, beta[p], NT, preferred_element_type=jnp.float32)
            ratio[p] = (wts[p] / denom).astype(jnp.bfloat16)

    def contribution():
        value = jnp.dot(ratio[0], beta[0], preferred_element_type=jnp.float32)
        value = value + jnp.dot(ratio[1], beta[1], preferred_element_type=jnp.float32)
        value = value + jnp.dot(ratio[2], beta[2], preferred_element_type=jnp.float32)
        return theta[...].astype(jnp.float32) * value

    def update(t):
        divide()
        gbuf[t] = alp[t] + contribution()
        expect(t, 0, 1)

    def statistics(t):
        th = theta[...]
        scale = float(2 ** (t + 3))
        for p in range(3):
            stat = lax.dot_general(ratio[p], th, TN, preferred_element_type=jnp.float32)
            for i in range(4):
                piece = beta[p, i * HALF : (i + 1) * HALF, :].astype(jnp.float32) * stat[i * HALF : (i + 1) * HALF, :]
                part[(t * (SLOTS + 1)) * 2 + p * 4 + i] = piece.astype(jnp.bfloat16).astype(jnp.float32) * scale

    acc = jnp.zeros((32, TOPICS), jnp.float32)
    for i in range(chunks):
        lam_copy(i).wait()

        def add_rows(n, acc, i=i):
            value = lam[i * rows + n]
            return acc + (value[:32] + value[32:])

        acc = lax.fori_loop(0, rows, add_rows, acc)
    sums = jnp.sum(acc, axis=0, keepdims=True)
    for copy in own_ids:
        copy.wait()
    for copy in own_docs:
        copy.wait()
    doc_prior(0)
    pl.semaphore_wait(barrier, len(peers))
    sum_start(0, sums)
    for t in range(1, STRATA):
        for copy in id_moves(t):
            copy.start()
    feat_move().start()
    cnt_move(2, 0).start()
    cnt_move(1, 0).start()
    exp_psi(0)
    zero = jnp.zeros((HALF, TOPICS), jnp.float32)
    for s in range(STRATA):
        for h in range(2):
            part[(s * (SLOTS + 1) + SLOTS) * 2 + h] = zero
    for h in range(2):
        rows_arriving(0, h)
        expect(0, h)
    weigh(0)
    alp_move(1).start()
    feat_move().wait_recv()
    next_feat = pltpu.make_async_copy(featv, feat, in_sem.at[2])
    next_feat.start()
    find_slots(0)
    for t in range(1, STRATA):
        for copy in id_moves(t):
            copy.wait_recv()
        local = [
            pltpu.make_async_copy(colv.at[t], cols.at[t], in_sem.at[0]),
            pltpu.make_async_copy(livv.at[t], live.at[t], in_sem.at[1]),
        ]
        for copy in local:
            copy.start()
        for copy in local:
            copy.wait()
    rows_staying(0)
    totals = sum_end(0)

    for t in range(STRATA):
        scale_beta(totals)
        lax.fori_loop(0, LOCAL, lambda n, carry, t=t: (update(t), carry)[1], 0)
        if t != 1:
            for h in range(2):
                gam_move(t, h).start()
        divide()
        if t + 1 < STRATA:
            sum_start(t + 1, jnp.sum(contribution(), axis=0, keepdims=True))
        if t == 0:
            cnt_move(2, 1).start()
            cnt_move(3, 0).start()
        if t == 1:
            for h in range(2):
                gam_move(t, h).start()
            cnt_move(3, 1).start()
        statistics(t)
        if t + 1 < STRATA:
            exp_psi(t + 1)
            find_slots(t + 1)
            if t == 0:
                next_feat.wait()
                doc_prior(2)
                alp_move(3).start()
            if t != 1:
                alp_move(t + 1).wait_recv()
            for n in range(len(PIECES[t + 1])):
                cnt_move(t + 1, n).wait_recv()
            weigh(t + 1)
            for h in range(2):
                gam_move(t, h).wait_recv()
                rows_arriving(t + 1, h)
                expect(t + 1, h)
            rows_staying(t + 1)
            totals = 0.5 * totals + 0.5 * (WORD_PRIOR * VOCAB + GROUPS * sum_end(t + 1))

    give = 1 - zh
    keep = zh
    ups = (FWD_F, MRG_F, UNM_K)
    ODD = 3

    def rs_copy(kind, i):
        to = across if kind == ACROSS else up if kind in ups else down
        return pltpu.make_async_remote_copy(rbuf.at[kind, i], rrecv.at[kind, i], rs_s.at[kind, i], rs_r.at[kind, i], device_id=to, device_id_type=MESH)

    def odd_copy(kind, h):
        if kind == FWD_F:
            return pltpu.make_async_remote_copy(rbuf.at[kind, ODD], rrecv.at[kind, ODD], rs_s.at[kind, ODD], rs_r.at[kind, ODD], device_id=across, device_id_type=MESH)
        rows_h = pl.ds(h * HALF, HALF)
        to = up if (kind == UNM_K) != (h == 1) else down
        return pltpu.make_async_remote_copy(rbuf.at[kind, ODD, rows_h], rrecv.at[kind, ODD, rows_h], rs_s.at[kind, ODD + h], rs_r.at[kind, ODD + h], device_id=to, device_id_type=MESH)

    def gathered(side, step, i, h):
        c = side * 16 + ((y + step) % NY) * 4 + i
        value = part[inv[0, c] * 2 + h]
        for s in range(1, STRATA):
            value = value + part[(s * (SLOTS + 1) + inv[s, c]) * 2 + h]
        return value

    def fill(kind, i, side, step, h, received=()):
        part_rows = pl.ds(h * HALF, HALF)
        value = gathered(side, step, i, h)
        for other in received:
            value = value + rrecv[other, i, part_rows, :]
        rbuf[kind, i, part_rows, :] = value

    def put(kind, i, side, step, received=()):
        for other in received:
            rs_copy(other, i).wait_recv()
        for h in range(2):
            fill(kind, i, side, step, h, received)
        rs_copy(kind, i).start()

    def first_three(body):
        lax.fori_loop(0, ODD, lambda i, carry: (body(i), carry)[1], 0)

    def merge_give(i):
        put(MRG_F, i, give, 1, (FWD_F,))

    def merge_keep(i):
        put(MRG_K, i, keep, 3, (FWD_K,))

    def send_across(i):
        put(ACROSS, i, give, 0, (UNM_F, MRG_F))

    for h in range(2):
        fill(FWD_F, ODD, give, 2, h)
    odd_copy(FWD_F, 0).start()
    put(MRG_F, ODD, give, 1)
    put(UNM_F, ODD, give, 3)
    for i in (0, 1):
        put(FWD_F, i, give, 2)
        put(UNM_F, i, give, 3)
    put(UNM_F, 2, give, 3)
    first_three(lambda i: put(FWD_K, i, keep, 2))
    send_across(ODD)
    merge_give(0)
    put(FWD_F, 2, give, 2)
    merge_give(1)
    send_across(0)
    merge_give(2)
    odd_copy(FWD_F, 0).wait_recv()
    for h in range(2):
        fill(FWD_K, ODD, keep, 2, h, (FWD_F,))
        odd_copy(FWD_K, h).start()
    first_three(lambda i: put(UNM_K, i, keep, 1))
    for h in range(2):
        fill(UNM_K, ODD, keep, 1 + 2 * h, h)
        odd_copy(UNM_K, h).start()
    merge_keep(0)
    send_across(1)
    merge_keep(1)
    merge_keep(2)
    send_across(2)
    for h in range(2):
        odd_copy(FWD_K, h).wait_recv()
        fill(MRG_K, ODD, keep, 3 - 2 * h, h, (FWD_K,))
        odd_copy(MRG_K, h).start()
    for h in range(2):
        gam_move(STRATA - 1, h).wait_recv()
    gout[...] = gbuf[STRATA]

    def finish(i):
        for h in range(2):
            part_rows = pl.ds(h * HALF, HALF)
            value = gathered(keep, 0, i, h)
            for kind in (UNM_K, MRG_K, ACROSS):
                value = value + rrecv[kind, i, part_rows, :]
            start = lam[(grp * 4 + i) * 2 + h]
            lout[i, part_rows, :] = start * 0.0625 + (value * (1.0 / 128.0) + WORD_PRIOR * 0.9375)

    def last_round(i):
        for kind in (UNM_K, MRG_K, ACROSS):
            rs_copy(kind, i).wait_recv()
        finish(i)

    first_three(last_round)
    for h in range(2):
        odd_copy(UNM_K, h).wait_recv()
        odd_copy(MRG_K, h).wait_recv()
    rs_copy(ACROSS, ODD).wait_recv()
    finish(ODD)

    for r in range(STRATA):
        sum_wait(r, ar_s)
        for h in range(2):
            gam_move(r, h).wait_send()
        if r > 0:
            if r == 2:
                feat_move().wait_send()
            else:
                alp_move(r).wait_send()
            for n in range(len(PIECES[r])):
                cnt_move(r, n).wait_send()
            for copy in id_moves(r):
                copy.wait_send()

    def drain(i):
        for kind in range(7):
            rs_copy(kind, i).wait_send()

    first_three(drain)
    for kind in (MRG_F, UNM_F, ACROSS):
        rs_copy(kind, ODD).wait_send()
    odd_copy(FWD_F, 0).wait_send()
    for kind in (FWD_K, MRG_K, UNM_K):
        for h in range(2):
            odd_copy(kind, h).wait_send()


def on_device(lambda_init, gamma_init, dmr_table, features, counts, tile_cols, live_slots):
    hbm = pl.BlockSpec(memory_space=pl.ANY)
    vmem = pl.BlockSpec(memory_space=pltpu.VMEM)
    f32, bf16, i32 = jnp.float32, jnp.bfloat16, jnp.int32
    dma = pltpu.SemaphoreType.DMA
    doc = (TILE, TOPICS)
    gamma_out, lambda_out = pl.pallas_call(
        kernel,
        out_shape=(pltpu.VMEM(doc, f32), pltpu.VMEM((4,) + doc, f32)),
        in_specs=[hbm] * 7,
        out_specs=(vmem, vmem),
        scratch_shapes=[
            pltpu.VMEM((2 * COLS, HALF, TOPICS), f32),
            pltpu.VMEM((1024, TOPICS), f32),
            pltpu.VMEM((STRATA, SLOTS, TILE, TILE), i32),
            pltpu.VMEM((STRATA,) + doc, f32),
            pltpu.VMEM((STRATA + 1,) + doc, f32),
            pltpu.VMEM((3, TILE, 2 * TILE), f32),
            pltpu.VMEM((2 * SLOTS, HALF, TOPICS), f32),
            pltpu.VMEM((3, 2 * TILE, TOPICS), bf16),
            pltpu.VMEM(doc, bf16),
            pltpu.VMEM((TILE, TILE), f32),
            pltpu.VMEM((3, TILE, 2 * TILE), bf16),
            pltpu.VMEM((STRATA * (SLOTS + 1) * 2, HALF, TOPICS), f32),
            pltpu.VMEM((STRATA, STRATA, SLOTS), i32),
            pltpu.VMEM((STRATA, 1, STRATA), i32),
            pltpu.VMEM((4, TILE), i32),
            pltpu.SMEM((4, TILE), i32),
            pltpu.SMEM((STRATA, STRATA, SLOTS), i32),
            pltpu.SMEM((STRATA, 1, STRATA), i32),
            pltpu.SMEM((STRATA, COLS), i32),
            pltpu.VMEM((STRATA, 1, TOPICS), f32),
            pltpu.VMEM((STRATA, len(FAR_FIRST), 1, TOPICS), f32),
            pltpu.VMEM((7, 4) + doc, f32),
            pltpu.VMEM((7, 4) + doc, f32),
            dma((4,)),
            dma((6,)),
            dma((STRATA, 2)),
            dma((STRATA, 2)),
            dma((STRATA,)),
            dma((STRATA,)),
            dma((20,)),
            dma((20,)),
            dma((7, 5)),
            dma((7, 5)),
        ],
        compiler_params=pltpu.CompilerParams(collective_id=0, has_side_effects=True),
        name="strata",
    )(
        lambda_init.reshape(2 * COLS, HALF, TOPICS),
        counts[0],
        gamma_init,
        dmr_table,
        features.T,
        tile_cols[0],
        live_slots,
    )
    return gamma_out, lambda_out.reshape(4 * TILE, TOPICS)


def solution(mesh):
    placed = (
        P("blk", None),
        P(("blk", "grp"), None),
        P(),
        P(("blk", "grp"), None),
        P(("blk", "grp"), None, None, None, None),
        P(("blk", "grp"), None, None),
        P(("blk", "grp"), None),
    )
    return jax.shard_map(
        on_device,
        mesh=mesh,
        in_specs=placed,
        out_specs=(P(("blk", "grp"), None), P(("blk", "grp"), None)),
        check_vma=False,
    )
```

```python
import jax
import jax.numpy as jnp
from jax import lax
from jax.experimental import pallas as pl
from jax.experimental.pallas import tpu as pltpu
from jax.sharding import PartitionSpec as P

STRATA = 4
LOCAL = 3
ORDER = (0, 1, 3, 2)
SLOTS = 6
TILE = 128
HALF = 64
TOPICS = 256
COLS = 32
VOCAB = 131072
GROUPS = 8
WORD_PRIOR = 0.05
NX, NZ, NY = 4, 4, 4
MESH = pl.DeviceIdType.MESH
NT = (((1,), (1,)), ((), ()))
TN = (((0,), (0,)), ((), ()))
PIECES = ((), ((0, 6),), ((0, 5), (5, 1)), ((0, 3), (3, 3)))
FWD_F, UNM_F, FWD_K, MRG_F, UNM_K, MRG_K, ACROSS = range(7)
FAR_FIRST = sorted(range(1, 2 * NX * NZ), key=lambda k: -(min(k // 2 % NX, NX - k // 2 % NX) + min(k // (2 * NX), NZ - k // (2 * NX))))


def flip(value, bits):
    if bits & 1:
        value = value + 1 - 2 * (value % 2)
    if bits & 2:
        value = value + 2 - 4 * ((value // 2) % 2)
    return value


def psi_parts(x):
    q = x * (x + 3.0)
    d = q * (q + 2.0)
    v = x + 3.5
    r = 1.0 / (v * d)
    rv = r * d
    second = 4.0 * ((x + 1.5) * (q + 1.0) * (r * v))
    r2 = rv * rv
    first = v + rv * (1.0 / 24.0 + r2 * (-37.0 / 5760.0 + r2 * (10313.0 / 2903040.0)))
    return first, second


def minus_psi(x):
    q = x * (x + 3.0)
    v = x + 3.5
    rv = 1.0 / v
    second = 4.0 * ((x + 1.5) * (q + 1.0)) * (1.0 / (q * (q + 2.0)))
    r2 = rv * rv
    first = v + rv * (1.0 / 24.0 + r2 * (-37.0 / 5760.0 + r2 * (10313.0 / 2903040.0)))
    return second - jnp.log(first)


def kernel(
    lam_any, cnt_any, gam_any, tab_any, feat_any, cols_any, live_any,
    gout, lout,
    lam, tab, cnt, alp, gbuf, wts, ebuf, beta, theta, rows_log, ratio, part, colv, livv, featv, feat, cols, live, inv,
    ar_src, ar_dst, rbuf, rrecv,
    lam_sem, in_sem, id_s, id_r, ar_s, ar_r, mv_s, mv_r, rs_s, rs_r,
):
    blk = lax.axis_index("blk")
    grp = lax.axis_index("grp")
    core = blk % 2
    x = (blk // 2) % NX
    z = blk // (2 * NX)
    y = grp % NY
    zh = grp // NY

    def other(k):
        side = core + 1 - 2 * core if k % 2 else core
        return ((((z + k // (2 * NX)) % NZ) * NX + (x + (k // 2) % NX) % NX) * 2 + side, grp)

    others = [other(k) for k in FAR_FIRST]

    def flipped(bits):
        return (flip(blk, bits), grp)

    up = (blk, zh * NY + (y + 1) % NY)
    down = (blk, zh * NY + (y + NY - 1) % NY)
    across = (blk, (1 - zh) * NY + y)
    peers = others + [up, down, across]

    barrier = pltpu.get_barrier_semaphore()
    for peer in peers:
        pl.semaphore_signal(barrier, inc=1, device_id=peer, device_id_type=MESH)

    chunks = 4
    rows = 2 * COLS // chunks

    def lam_copy(i):
        return pltpu.make_async_copy(lam_any.at[pl.ds(i * rows, rows)], lam.at[pl.ds(i * rows, rows)], lam_sem.at[i])

    own_ids = [
        pltpu.make_async_copy(cols_any, cols.at[0], in_sem.at[0]),
        pltpu.make_async_copy(live_any, live.at[0], in_sem.at[1]),
    ]
    own_docs = [
        pltpu.make_async_copy(feat_any, feat, in_sem.at[2]),
        pltpu.make_async_copy(tab_any, tab, in_sem.at[3]),
        pltpu.make_async_copy(cnt_any.at[0], cnt.at[0], in_sem.at[4]),
        pltpu.make_async_copy(gam_any, gbuf.at[0], in_sem.at[5]),
    ]
    for copy in own_ids:
        copy.start()
    for i in range(chunks):
        lam_copy(i).start()
    for copy in own_docs:
        copy.start()

    def move(src, dst, n, bits):
        return pltpu.make_async_remote_copy(src, dst, mv_s.at[n], mv_r.at[n], device_id=flipped(bits), device_id_type=MESH)

    def cnt_move(t, n):
        tiles = pl.ds(*PIECES[t][n])
        return move(cnt_any.at[t, tiles], cnt.at[t, tiles], 3 * (t - 1) + n, ORDER[t])

    def alp_move(t):
        return move(alp.at[t - 1], alp.at[t], 8 + t, ORDER[t - 1] ^ ORDER[t])

    def feat_move():
        return move(feat_any, featv, 10, ORDER[2])

    def gam_move(t, h):
        bits = ORDER[t] ^ (ORDER[t + 1] if t + 1 < STRATA else 0)
        rows_h = pl.ds(h * HALF, HALF)
        return move(gbuf.at[t, rows_h], gbuf.at[t + 1, rows_h], 12 + 2 * t + h, bits)

    def id_moves(t):
        return [
            pltpu.make_async_remote_copy(cols_any, colv.at[t], id_s.at[t, 0], id_r.at[t, 0], device_id=flipped(ORDER[t]), device_id_type=MESH),
            pltpu.make_async_remote_copy(live_any, livv.at[t], id_s.at[t, 1], id_r.at[t, 1], device_id=flipped(ORDER[t]), device_id_type=MESH),
        ]

    def sum_start(r, value):
        ar_src[r] = value
        for k, peer in enumerate(others):
            pltpu.make_async_remote_copy(ar_src.at[r], ar_dst.at[r, k], ar_s.at[r], ar_r.at[r], device_id=peer, device_id_type=MESH).start()

    def sum_wait(r, sem):
        pltpu.make_async_copy(ar_dst.at[r], ar_dst.at[r], sem.at[r]).wait()

    def sum_end(r):
        sum_wait(r, ar_r)
        parts = [ar_src[r]] + [ar_dst[r, k] for k in range(len(others))]
        while len(parts) > 1:
            parts = [sum(parts[i + 1 : i + 2], parts[i]) for i in range(0, len(parts), 2)]
        return parts[0]

    def find_slots(s):
        ids = [cols[s, s, j] for j in range(SLOTS)]

        def column(i, carry):
            for n in range(4):
                c = i * 4 + n
                slot = SLOTS
                for j in range(SLOTS):
                    slot = jnp.where(ids[j] == c, j, slot)
                inv[s, c] = slot
            return carry

        lax.fori_loop(0, COLS // 4, column, 0)

    def exp_psi(t):
        decay = 0.5**t
        offset = WORD_PRIOR * (1.0 - decay)

        def tile_half(i, carry):
            c = cols[t, t, i // 2]
            h = i % 2
            value = lam[c * 2 + h]
            for s in range(t):
                value = value + part[(s * (SLOTS + 1) + inv[s, c]) * 2 + h]
            first, second = psi_parts(value * decay + offset)
            ebuf[i] = first * jnp.exp(-second)
            return carry

        lax.fori_loop(0, 2 * SLOTS, tile_half, 0)

    def weigh(t):
        used = live[t, 0, t]
        for j in range(SLOTS):
            keep = jnp.where(j < used, 1.0, 0.0).astype(jnp.float32)
            wts[j // 2, :, (j % 2) * TILE : (j % 2 + 1) * TILE] = cnt[t, j].astype(jnp.float32) * keep

    def scale_beta(totals):
        v = totals - 0.5
        scale = v / (v * v + 1.0 / 24.0)
        for i in range(2 * SLOTS):
            beta[i // 4, (i % 4) * HALF : (i % 4 + 1) * HALF, :] = (ebuf[i] * scale).astype(jnp.bfloat16)

    def doc_prior(t):
        def eight(b, carry):
            for r in range(8):
                n = b * 8 + r
                value = tab[pl.ds(feat[0, n], 1), :]
                for f in range(1, 4):
                    value = value + tab[pl.ds(feat[f, n], 1), :]
                alp[t, pl.ds(n, 1), :] = value
            return carry

        lax.fori_loop(0, TILE // 8, eight, 0)
        for h in range(2):
            alp[t, h * HALF : (h + 1) * HALF, :] = jnp.exp(alp[t, h * HALF : (h + 1) * HALF, :])

    def row_sum(value):
        return jnp.sum(value, axis=1, keepdims=True)

    def set_rows(sums, h):
        rows_log[h * HALF : (h + 1) * HALF, :] = jnp.broadcast_to(minus_psi(sums), (HALF, TILE))

    def rows_arriving(t, h):
        set_rows(row_sum(gbuf[t, h * HALF : (h + 1) * HALF, :]), h)

    def rows_staying(t):
        for h in range(2):
            docs = slice(h * HALF, (h + 1) * HALF)
            set_rows(row_sum(alp[t, docs, :]) + row_sum(wts[0, docs, :] + wts[1, docs, :] + wts[2, docs, :]), h)

    def expect(t, *halves):
        for h in halves:
            docs = slice(h * HALF, (h + 1) * HALF)
            log_row = rows_log[docs, :]
            for side in range(2):
                topics = slice(side * TILE, (side + 1) * TILE)
                first, second = psi_parts(gbuf[t, docs, topics])
                theta[docs, topics] = (first * jnp.exp(log_row - second)).astype(jnp.bfloat16)

    def divide():
        th = theta[...]
        for p in range(3):
            denom = lax.dot_general(th, beta[p], NT, preferred_element_type=jnp.float32)
            ratio[p] = (wts[p] / denom).astype(jnp.bfloat16)

    def contribution():
        value = jnp.dot(ratio[0], beta[0], preferred_element_type=jnp.float32)
        value = value + jnp.dot(ratio[1], beta[1], preferred_element_type=jnp.float32)
        value = value + jnp.dot(ratio[2], beta[2], preferred_element_type=jnp.float32)
        return theta[...].astype(jnp.float32) * value

    def update(t):
        divide()
        gbuf[t] = alp[t] + contribution()
        expect(t, 0, 1)

    def statistics(t):
        th = theta[...]
        scale = float(2 ** (t + 3))
        for p in range(3):
            stat = lax.dot_general(ratio[p], th, TN, preferred_element_type=jnp.float32)
            for i in range(4):
                piece = beta[p, i * HALF : (i + 1) * HALF, :].astype(jnp.float32) * stat[i * HALF : (i + 1) * HALF, :]
                part[(t * (SLOTS + 1)) * 2 + p * 4 + i] = piece.astype(jnp.bfloat16).astype(jnp.float32) * scale

    acc = jnp.zeros((32, TOPICS), jnp.float32)
    for i in range(chunks):
        lam_copy(i).wait()

        def add_rows(n, acc, i=i):
            value = lam[i * rows + n]
            return acc + (value[:32] + value[32:])

        acc = lax.fori_loop(0, rows, add_rows, acc)
    sums = jnp.sum(acc, axis=0, keepdims=True)
    for copy in own_ids:
        copy.wait()
    for copy in own_docs:
        copy.wait()
    doc_prior(0)
    find_slots(0)
    pl.semaphore_wait(barrier, len(peers))
    sum_start(0, sums)
    for t in range(1, STRATA):
        for copy in id_moves(t):
            copy.start()
    feat_move().start()
    cnt_move(2, 0).start()
    cnt_move(1, 0).start()
    exp_psi(0)
    zero = jnp.zeros((HALF, TOPICS), jnp.float32)
    for s in range(STRATA):
        for h in range(2):
            part[(s * (SLOTS + 1) + SLOTS) * 2 + h] = zero
    for h in range(2):
        rows_arriving(0, h)
        expect(0, h)
    weigh(0)
    alp_move(1).start()
    feat_move().wait_recv()
    next_feat = pltpu.make_async_copy(featv, feat, in_sem.at[2])
    next_feat.start()
    for t in range(1, STRATA):
        for copy in id_moves(t):
            copy.wait_recv()
        local = [
            pltpu.make_async_copy(colv.at[t], cols.at[t], in_sem.at[0]),
            pltpu.make_async_copy(livv.at[t], live.at[t], in_sem.at[1]),
        ]
        for copy in local:
            copy.start()
        for copy in local:
            copy.wait()
    rows_staying(0)
    totals = sum_end(0)

    for t in range(STRATA):
        scale_beta(totals)
        lax.fori_loop(0, LOCAL, lambda n, carry, t=t: (update(t), carry)[1], 0)
        if t != 1:
            for h in range(2):
                gam_move(t, h).start()
        divide()
        if t + 1 < STRATA:
            sum_start(t + 1, jnp.sum(contribution(), axis=0, keepdims=True))
        if t == 0:
            cnt_move(2, 1).start()
            cnt_move(3, 0).start()
        if t == 1:
            for h in range(2):
                gam_move(t, h).start()
            cnt_move(3, 1).start()
        statistics(t)
        if t + 1 < STRATA:
            exp_psi(t + 1)
            find_slots(t + 1)
            if t == 0:
                next_feat.wait()
                doc_prior(2)
                alp_move(3).start()
            if t != 1:
                alp_move(t + 1).wait_recv()
            for n in range(len(PIECES[t + 1])):
                cnt_move(t + 1, n).wait_recv()
            weigh(t + 1)
            for h in range(2):
                gam_move(t, h).wait_recv()
                rows_arriving(t + 1, h)
                expect(t + 1, h)
            rows_staying(t + 1)
            totals = 0.5 * totals + 0.5 * (WORD_PRIOR * VOCAB + GROUPS * sum_end(t + 1))

    give = 1 - zh
    keep = zh
    ups = (FWD_F, MRG_F, UNM_K)
    ODD = 3

    def rs_copy(kind, i):
        to = across if kind == ACROSS else up if kind in ups else down
        return pltpu.make_async_remote_copy(rbuf.at[kind, i], rrecv.at[kind, i], rs_s.at[kind, i], rs_r.at[kind, i], device_id=to, device_id_type=MESH)

    def odd_copy(kind, h):
        if kind == FWD_F:
            return pltpu.make_async_remote_copy(rbuf.at[kind, ODD], rrecv.at[kind, ODD], rs_s.at[kind, ODD], rs_r.at[kind, ODD], device_id=across, device_id_type=MESH)
        rows_h = pl.ds(h * HALF, HALF)
        to = up if (kind == UNM_K) != (h == 1) else down
        return pltpu.make_async_remote_copy(rbuf.at[kind, ODD, rows_h], rrecv.at[kind, ODD, rows_h], rs_s.at[kind, ODD + h], rs_r.at[kind, ODD + h], device_id=to, device_id_type=MESH)

    def gathered(side, step, i, h):
        c = side * 16 + ((y + step) % NY) * 4 + i
        value = part[inv[0, c] * 2 + h]
        for s in range(1, STRATA):
            value = value + part[(s * (SLOTS + 1) + inv[s, c]) * 2 + h]
        return value

    def fill(kind, i, side, step, h, received=()):
        part_rows = pl.ds(h * HALF, HALF)
        value = gathered(side, step, i, h)
        for other in received:
            value = value + rrecv[other, i, part_rows, :]
        rbuf[kind, i, part_rows, :] = value

    def put(kind, i, side, step, received=()):
        for other in received:
            rs_copy(other, i).wait_recv()
        for h in range(2):
            fill(kind, i, side, step, h, received)
        rs_copy(kind, i).start()

    def first_three(body):
        lax.fori_loop(0, ODD, lambda i, carry: (body(i), carry)[1], 0)

    def merge_give(i):
        put(MRG_F, i, give, 1, (FWD_F,))

    def merge_keep(i):
        put(MRG_K, i, keep, 3, (FWD_K,))

    def send_across(i):
        put(ACROSS, i, give, 0, (UNM_F, MRG_F))

    for h in range(2):
        fill(FWD_F, ODD, give, 2, h)
    odd_copy(FWD_F, 0).start()
    put(MRG_F, ODD, give, 1)
    put(UNM_F, ODD, give, 3)
    for i in (0, 1):
        put(FWD_F, i, give, 2)
        put(UNM_F, i, give, 3)
    put(UNM_F, 2, give, 3)
    first_three(lambda i: put(FWD_K, i, keep, 2))
    send_across(ODD)
    merge_give(0)
    put(FWD_F, 2, give, 2)
    merge_give(1)
    send_across(0)
    merge_give(2)
    odd_copy(FWD_F, 0).wait_recv()
    for h in range(2):
        fill(FWD_K, ODD, keep, 2, h, (FWD_F,))
        odd_copy(FWD_K, h).start()
    first_three(lambda i: put(UNM_K, i, keep, 1))
    for h in range(2):
        fill(UNM_K, ODD, keep, 1 + 2 * h, h)
        odd_copy(UNM_K, h).start()
    merge_keep(0)
    send_across(1)
    merge_keep(1)
    merge_keep(2)
    send_across(2)
    for h in range(2):
        odd_copy(FWD_K, h).wait_recv()
        fill(MRG_K, ODD, keep, 3 - 2 * h, h, (FWD_K,))
        odd_copy(MRG_K, h).start()
    for h in range(2):
        gam_move(STRATA - 1, h).wait_recv()
    gout[...] = gbuf[STRATA]

    def finish(i):
        for h in range(2):
            part_rows = pl.ds(h * HALF, HALF)
            value = gathered(keep, 0, i, h)
            for kind in (UNM_K, MRG_K, ACROSS):
                value = value + rrecv[kind, i, part_rows, :]
            start = lam[(grp * 4 + i) * 2 + h]
            lout[i, part_rows, :] = start * 0.0625 + (value * (1.0 / 128.0) + WORD_PRIOR * 0.9375)

    def last_round(i):
        for kind in (UNM_K, MRG_K, ACROSS):
            rs_copy(kind, i).wait_recv()
        finish(i)

    first_three(last_round)
    for h in range(2):
        odd_copy(UNM_K, h).wait_recv()
        odd_copy(MRG_K, h).wait_recv()
    rs_copy(ACROSS, ODD).wait_recv()
    finish(ODD)

    for r in range(STRATA):
        sum_wait(r, ar_s)
        for h in range(2):
            gam_move(r, h).wait_send()
        if r > 0:
            if r == 2:
                feat_move().wait_send()
            else:
                alp_move(r).wait_send()
            for n in range(len(PIECES[r])):
                cnt_move(r, n).wait_send()
            for copy in id_moves(r):
                copy.wait_send()

    def drain(i):
        for kind in range(7):
            rs_copy(kind, i).wait_send()

    first_three(drain)
    for kind in (MRG_F, UNM_F, ACROSS):
        rs_copy(kind, ODD).wait_send()
    odd_copy(FWD_F, 0).wait_send()
    for kind in (FWD_K, MRG_K, UNM_K):
        for h in range(2):
            odd_copy(kind, h).wait_send()


def on_device(lambda_init, gamma_init, dmr_table, features, counts, tile_cols, live_slots):
    hbm = pl.BlockSpec(memory_space=pl.ANY)
    vmem = pl.BlockSpec(memory_space=pltpu.VMEM)
    f32, bf16, i32 = jnp.float32, jnp.bfloat16, jnp.int32
    dma = pltpu.SemaphoreType.DMA
    doc = (TILE, TOPICS)
    gamma_out, lambda_out = pl.pallas_call(
        kernel,
        out_shape=(pltpu.VMEM(doc, f32), pltpu.VMEM((4,) + doc, f32)),
        in_specs=[hbm] * 7,
        out_specs=(vmem, vmem),
        scratch_shapes=[
            pltpu.VMEM((2 * COLS, HALF, TOPICS), f32),
            pltpu.VMEM((1024, TOPICS), f32),
            pltpu.VMEM((STRATA, SLOTS, TILE, TILE), i32),
            pltpu.VMEM((STRATA,) + doc, f32),
            pltpu.VMEM((STRATA + 1,) + doc, f32),
            pltpu.VMEM((3, TILE, 2 * TILE), f32),
            pltpu.VMEM((2 * SLOTS, HALF, TOPICS), f32),
            pltpu.VMEM((3, 2 * TILE, TOPICS), bf16),
            pltpu.VMEM(doc, bf16),
            pltpu.VMEM((TILE, TILE), f32),
            pltpu.VMEM((3, TILE, 2 * TILE), bf16),
            pltpu.VMEM((STRATA * (SLOTS + 1) * 2, HALF, TOPICS), f32),
            pltpu.VMEM((STRATA, STRATA, SLOTS), i32),
            pltpu.VMEM((STRATA, 1, STRATA), i32),
            pltpu.VMEM((4, TILE), i32),
            pltpu.SMEM((4, TILE), i32),
            pltpu.SMEM((STRATA, STRATA, SLOTS), i32),
            pltpu.SMEM((STRATA, 1, STRATA), i32),
            pltpu.SMEM((STRATA, COLS), i32),
            pltpu.VMEM((STRATA, 1, TOPICS), f32),
            pltpu.VMEM((STRATA, len(FAR_FIRST), 1, TOPICS), f32),
            pltpu.VMEM((7, 4) + doc, f32),
            pltpu.VMEM((7, 4) + doc, f32),
            dma((4,)),
            dma((6,)),
            dma((STRATA, 2)),
            dma((STRATA, 2)),
            dma((STRATA,)),
            dma((STRATA,)),
            dma((20,)),
            dma((20,)),
            dma((7, 5)),
            dma((7, 5)),
        ],
        compiler_params=pltpu.CompilerParams(collective_id=0, has_side_effects=True),
        name="strata",
    )(
        lambda_init.reshape(2 * COLS, HALF, TOPICS),
        counts[0],
        gamma_init,
        dmr_table,
        features.T,
        tile_cols[0],
        live_slots,
    )
    return gamma_out, lambda_out.reshape(4 * TILE, TOPICS)


def solution(mesh):
    placed = (
        P("blk", None),
        P(("blk", "grp"), None),
        P(),
        P(("blk", "grp"), None),
        P(("blk", "grp"), None, None, None, None),
        P(("blk", "grp"), None, None),
        P(("blk", "grp"), None),
    )
    return jax.shard_map(
        on_device,
        mesh=mesh,
        in_specs=placed,
        out_specs=(P(("blk", "grp"), None), P(("blk", "grp"), None)),
        check_vma=False,
    )
```
